32 devices in a mesh: dp: 2 (over x), expert: 4 (over z), tensor: 4 (over y, core).
Axes of the slice: x: 2, y: 2, z: 4, core: 2. Of those that a mesh axis runs over, the one named last changes fastest.
Arguments:
- layer_input: bfloat16 [8192, 1536], P(('dp', 'expert', 'tensor')), may hold values from -6 to 6
- norm1_gain: float32 [1536], replicated, may hold values from 0.1 to 1.9
- w_query: bfloat16 [1536, 1536], P(None, 'tensor'), may hold values from -0.15625 to 0.15625
- key_matrix: bfloat16 [1536, 512], P(None, 'tensor'), may hold values from -0.15625 to 0.15625
- value_matrix: bfloat16 [1536, 512], P(None, 'tensor'), may hold values from -0.15625 to 0.15625
- w_out: bfloat16 [1536, 1536], P('tensor'), may hold values from -1.25 to 1.25
- norm2_gain: float32 [1536], replicated, may hold values from 0.1 to 1.9
- w_router: bfloat16 [1536, 20], replicated, may hold values from -0.078125 to 0.078125
- w_gate: bfloat16 [20, 1536, 512], P('expert', 'tensor'), may hold values from -0.15625 to 0.15625
- w_up: bfloat16 [20, 1536, 512], P('expert', 'tensor'), may hold values from -0.15625 to 0.15625
- w_down: bfloat16 [20, 512, 1536], P('expert', 'tensor'), may hold values from -0.5 to 0.5
- routes: int32 [8192, 8], P(('dp', 'expert', 'tensor')), may hold values from 0 to 19, all different within a row; in each aligned block of 256 rows (0 to 255, 256 to 511, ...) at most 128 rows name the same one
- cotangent: bfloat16 [8192, 1536], P(('dp', 'expert', 'tensor')), may hold values from -6 to 6
Outputs:
- layer_output: bfloat16 [8192, 1536], P(('dp', 'expert', 'tensor'))
- d_input: float32 [8192, 1536], P(('dp', 'expert', 'tensor'))
- d_norm1_gain: float32 [1536], replicated
- d_w_query: float32 [1536, 1536], P(None, 'tensor')
- d_w_key: float32 [1536, 512], P(None, 'tensor')
- d_w_value: float32 [1536, 512], P(None, 'tensor')
- d_w_out: float32 [1536, 1536], P('tensor')
- d_norm2_gain: float32 [1536], replicated
- d_w_router: float32 [1536, 20], replicated
- d_w_gate: float32 [20, 1536, 512], P('expert', 'tensor')
- d_w_up: float32 [20, 1536, 512], P('expert', 'tensor')
- d_w_down: float32 [20, 512, 1536], P('expert', 'tensor')
The draws below stay inside these ranges and needn't reach their ends.
Inputs may be any that keep to these rules, and one draw needn't show every extreme that they name: `routes`: each row names 8 different experts. In each aligned block of 256 rows (the rows of one device) no expert is named by more than 128 rows.
All inputs are finite; a program needn't handle non-finite values.
Results may differ from the reference program's by a relative error of at most 0.019.
Values may be sent and summed in bfloat16 or wider, within the bound.
No kernel may reach another device: no remote copies, remote signals or barrier semaphores. Data moves between devices by JAX's collectives and lax.ppermute only.
A program may use at most 256 MiB of HBM per device.

```python
import math
import jax
import jax.numpy as jnp
import numpy as np
from jax import lax

MODEL_WIDTH = 1536
QUERY_HEADS = 24
KEY_VALUE_HEADS = 8
HEAD_SIZE = 64
FFE = 512
TOPK = 8
SEQUENCE_TOKENS = 512
EXPERTS = 20
TOKENS = 8192
ROWS = 256
CAP = 128


def block_levels(stream_key, shape, shards, smallest, largest):
    def one(dim, shards_of):
        draws = jax.random.uniform(jax.random.fold_in(jax.random.fold_in(stream_key, 6), dim), (shards_of,), jnp.float32, smallest / len(shards), largest / len(shards))
        return jnp.repeat(jnp.exp(draws), shape[dim] // shards_of).reshape((-1,) + (1,) * (len(shape) - dim - 1))

    level = one(*shards[0])
    for cut in shards[1:]:
        level = level * one(*cut)
    return level


def assign_block(own_key, own, number, rows, amount, top, most, slope):
    order = jax.random.permutation(own_key, amount)
    packed, ordinary = portions_of(amount, rows * top, most, slope, True), portions_of(amount, rows * top, most, slope, False)
    places = jnp.arange(amount)

    def named(tallies, offset_by):
        used = int((tallies > 0).sum())
        fixed = max(1, used // 4)
        shifted = fixed + (places - fixed + offset_by * (used - fixed)) % max(1, amount - fixed)
        return jnp.zeros((amount,), jnp.int32).at[order[jnp.where(places < fixed, places, shifted)]].set(jnp.asarray(tallies, jnp.int32))

    tallies = jnp.where(number % 4 == 0, named(packed, number // 4), named(ordinary, number - number // 4 - 1))
    mixed = jax.random.permutation(jax.random.fold_in(own, 3), amount)
    source_of, receiver = mixed[0:amount // 2 * 2:2], mixed[1:amount // 2 * 2:2]
    room = jnp.minimum(tallies[source_of] - 1, most - tallies[receiver]) // 2
    room = jnp.where((source_of == order[0]) | (receiver == order[0]) | (tallies[receiver] == 0), 0, jnp.maximum(room, 0))
    shifted = jax.random.randint(jax.random.fold_in(own, 4), (amount // 2,), 0, 1 << 20) % (room + 1)
    tallies = tallies.at[source_of].add(-shifted).at[receiver].add(shifted)
    members = jnp.searchsorted(jnp.cumsum(tallies), jnp.arange(rows * top), side="right").astype(jnp.int32)
    listing = members.reshape(top, rows).T
    listing = listing[jax.random.permutation(jax.random.fold_in(own, 1), rows)]
    offset_by = jax.random.randint(jax.random.fold_in(own, 2), (rows, 1), 0, top)
    return jnp.take_along_axis(listing, (jnp.arange(top)[None, :] + offset_by) % top, axis=1)


def portions_of(number_of, total, most, lean, full):
    loads = [(1 << 20) // math.isqrt(grade ** lean) + 1 for grade in range(1, number_of + 1)]
    largest = most if full else min(most, max(-(-total // number_of), total * loads[0] // sum(loads)))
    least = 1 if total - largest >= number_of - 1 else 0
    counts, surplus = [largest] + [least] * (number_of - 1), total - largest - least * (number_of - 1)
    while surplus > 0:
        candidates = [i for i in range(1, number_of) if counts[i] < largest] or [i for i in range(1, number_of) if counts[i] < most]
        mass, budget = sum([loads[i] for i in candidates]), surplus
        for i in candidates:
            addition = min(most - counts[i], max(1, budget * loads[i] // mass), surplus)
            counts[i] = counts[i] + addition
            surplus = surplus - addition
    return np.array(counts)


def normal_values(rng, shape, scale, reach, split=(), kind=jnp.bfloat16):
    drawn = jax.random.normal(rng, shape, jnp.float32) * scale
    if len(split) > 0:
        drawn = block_levels(rng, shape, split, -0.22, 0.18) * drawn
    return jnp.clip(drawn, min=-reach, max=reach).astype(kind)


def setup_inputs(seed: int = 0) -> dict:
    splits = jax.random.split(jax.random.key(seed), 14)
    layer_input = normal_values(splits[0], (TOKENS, MODEL_WIDTH), 1.0, 6.0, ((0, 32),))
    norm1_gain = jnp.clip(1.0 + 0.18 * jax.random.normal(splits[1], (MODEL_WIDTH,), jnp.float32), 0.1, 1.9)
    w_query = normal_values(splits[2], (MODEL_WIDTH, QUERY_HEADS * HEAD_SIZE), MODEL_WIDTH ** -0.5, 0.15625, ((1, 4),))
    key_matrix = normal_values(splits[3], (MODEL_WIDTH, KEY_VALUE_HEADS * HEAD_SIZE), MODEL_WIDTH ** -0.5, 0.15625, ((1, 4),))
    value_matrix = normal_values(splits[4], (MODEL_WIDTH, KEY_VALUE_HEADS * HEAD_SIZE), MODEL_WIDTH ** -0.5, 0.15625, ((1, 4),))
    w_out = normal_values(splits[5], (QUERY_HEADS * HEAD_SIZE, MODEL_WIDTH), (QUERY_HEADS * HEAD_SIZE * 8 // SEQUENCE_TOKENS) ** -0.5, 1.25, ((0, 4),))
    norm2_gain = jnp.clip(1.0 + 0.18 * jax.random.normal(splits[6], (MODEL_WIDTH,), jnp.float32), 0.1, 1.9)
    w_router = normal_values(splits[7], (MODEL_WIDTH, EXPERTS), (MODEL_WIDTH * 4) ** -0.5, 0.078125)
    w_gate = normal_values(splits[8], (EXPERTS, MODEL_WIDTH, FFE), MODEL_WIDTH ** -0.5, 0.15625, ((0, 4), (1, 4)))
    w_up = normal_values(splits[9], (EXPERTS, MODEL_WIDTH, FFE), MODEL_WIDTH ** -0.5, 0.15625, ((0, 4), (1, 4)))
    w_down = normal_values(splits[10], (EXPERTS, FFE, MODEL_WIDTH), (FFE // 4) ** -0.5, 0.5, ((0, 4), (1, 4)))
    routes_keys = jax.random.split(jax.random.fold_in(splits[11], 1), TOKENS // ROWS)
    routes_turns = jax.random.permutation(jax.random.fold_in(splits[11], 3), TOKENS // ROWS)
    routes = jax.vmap(lambda own, number: assign_block(jax.random.fold_in(splits[11], 2), own, number, ROWS, EXPERTS, TOPK, CAP, 2))(routes_keys, routes_turns).reshape((TOKENS, TOPK))
    cotangent = normal_values(splits[12], (TOKENS, MODEL_WIDTH), 1.0, 6.0, ((0, 32),))
    return {"layer_input": layer_input, "norm1_gain": norm1_gain, "w_query": w_query, "key_matrix": key_matrix, "value_matrix": value_matrix, "w_out": w_out, "norm2_gain": norm2_gain, "w_router": w_router, "w_gate": w_gate, "w_up": w_up, "w_down": w_down, "routes": routes, "cotangent": cotangent}


EPS = 1e-06
THETA = 10000.0
HIGH = lax.Precision.HIGHEST

def rope_tables():
    half_size = HEAD_SIZE // 2
    freqs = jnp.exp(-jnp.log(THETA) * (2.0 * jnp.arange(half_size, dtype=jnp.float32)) / HEAD_SIZE)
    angles = jnp.arange(SEQUENCE_TOKENS, dtype=jnp.float32)[:, None] * freqs[None, :]
    return (jnp.cos(angles), jnp.sin(angles))

def rotate(tensor, cosine_table, sine_table):
    half_size = tensor.shape[-1] // 2
    first = tensor[..., :half_size]
    second = tensor[..., half_size:]
    return jnp.concatenate([first * cosine_table - second * sine_table, second * cosine_table + first * sine_table], axis=-1)

def unrotate_pairs(tensor, cosine_table, sine_table):
    half_size = tensor.shape[-1] // 2
    first = tensor[..., :half_size]
    second = tensor[..., half_size:]
    return jnp.concatenate([first * cosine_table + second * sine_table, second * cosine_table - first * sine_table], axis=-1)

def normalize(row_data):
    inverse = lax.rsqrt(lax.optimization_barrier(jnp.mean(row_data * row_data, axis=-1, keepdims=True)) + EPS)
    return (row_data * inverse, inverse)

def normalize_back(d_normed, normal_hat, inverse, gain):
    d_hat = d_normed * gain
    return inverse * (d_hat - normal_hat * lax.optimization_barrier(jnp.mean(d_hat * normal_hat, axis=-1, keepdims=True)))

def contract_first(left, right):
    return lax.dot_general(left, right, (((0,), (0,)), ((), ())), preferred_element_type=jnp.float32)

def contract_last(left, right):
    return lax.dot_general(left, right, (((1,), (1,)), ((), ())), preferred_element_type=jnp.float32)

def slot_tables(route_rows, expert_total, capacity):
    row_count, top_count = route_rows.shape
    flat_routes = route_rows.reshape(-1)
    one_hot = (flat_routes[:, None] == jnp.arange(expert_total, dtype=jnp.int32)[None, :]).astype(jnp.int32)
    earlier = jnp.cumsum(one_hot, axis=0) - one_hot
    place = lax.optimization_barrier(jnp.sum(earlier * one_hot, axis=1)).astype(jnp.int32)
    slot = (flat_routes * capacity + place).astype(jnp.int32)
    pair_total = row_count * top_count
    slot_pair = jnp.full((expert_total * capacity,), pair_total, jnp.int32).at[slot].set(jnp.arange(pair_total, dtype=jnp.int32))
    return (slot, slot_pair)

def attention_pieces(seq_rows, norm1_gain, w_query, key_matrix, value_matrix, w_out, cosine_table, sine_table):
    query_groups = QUERY_HEADS // KEY_VALUE_HEADS
    scale = 1.0 / math.sqrt(HEAD_SIZE)
    row_float = seq_rows.astype(jnp.float32)
    hat_one, inverse_one = normalize(row_float)
    first_normed_input = (hat_one * norm1_gain).astype(jnp.bfloat16)
    query_rows = jnp.dot(first_normed_input, w_query, preferred_element_type=jnp.float32)
    query_rows = query_rows.reshape(SEQUENCE_TOKENS, KEY_VALUE_HEADS, query_groups, HEAD_SIZE).transpose(1, 2, 0, 3)
    key_rows = jnp.dot(first_normed_input, key_matrix, preferred_element_type=jnp.float32).reshape(SEQUENCE_TOKENS, KEY_VALUE_HEADS, HEAD_SIZE).transpose(1, 0, 2)
    value_rows = jnp.dot(first_normed_input, value_matrix, preferred_element_type=jnp.float32).reshape(SEQUENCE_TOKENS, KEY_VALUE_HEADS, HEAD_SIZE).transpose(1, 0, 2)
    value_rows = value_rows.astype(jnp.bfloat16)
    query_rows = rotate(query_rows, cosine_table, sine_table).astype(jnp.bfloat16)
    key_rows = rotate(key_rows, cosine_table, sine_table).astype(jnp.bfloat16)
    positions = jnp.arange(SEQUENCE_TOKENS, dtype=jnp.int32)
    causal = positions[:, None] >= positions[None, :]
    scores = jnp.einsum('kgqd,kvd->kgqv', query_rows.astype(jnp.float32), key_rows.astype(jnp.float32)) * scale
    totals = lax.optimization_barrier(jnp.sum(jnp.where(causal, jnp.exp(scores), 0.0), axis=-1, keepdims=True))
    probs = jnp.where(causal, jnp.exp(scores - jnp.log(totals)), 0.0)
    probs_low = probs.astype(jnp.bfloat16)
    heads = jnp.einsum('kgqv,kvd->kgqd', probs_low.astype(jnp.float32), value_rows.astype(jnp.float32)).astype(jnp.bfloat16)
    heads_flat = heads.transpose(2, 0, 1, 3).reshape(SEQUENCE_TOKENS, QUERY_HEADS * HEAD_SIZE)
    hidden = row_float + jnp.dot(heads_flat, w_out, preferred_element_type=jnp.float32)
    return (hat_one, inverse_one, first_normed_input, query_rows, key_rows, value_rows, probs, probs_low, heads_flat, hidden)

def reference(layer_input, norm1_gain, w_query, key_matrix, value_matrix, w_out, norm2_gain, w_router, w_gate, w_up, w_down, routes, cotangent):
    cosine_table, sine_table = rope_tables()
    query_groups = QUERY_HEADS // KEY_VALUE_HEADS
    scale = 1.0 / math.sqrt(HEAD_SIZE)
    seq_count = TOKENS // SEQUENCE_TOKENS
    seq_input = layer_input.reshape(seq_count, SEQUENCE_TOKENS, MODEL_WIDTH)

    def forward_one(seq_rows):
        return attention_pieces(seq_rows, norm1_gain, w_query, key_matrix, value_matrix, w_out, cosine_table, sine_table)[9]
    hidden_all = lax.map(forward_one, seq_input).reshape(TOKENS, MODEL_WIDTH)
    gate_float = w_gate.astype(jnp.float32)
    up_float = w_up.astype(jnp.float32)
    down_float = w_down.astype(jnp.float32)
    expert_ids = jnp.arange(EXPERTS, dtype=jnp.int32)

    def moe_block(carry, inputs):
        grad_norm2, grad_router, grad_gate, grad_up, grad_down = carry
        hidden_rows, route_rows, cot_rows = inputs
        hat_two, inverse_two = normalize(hidden_rows)
        normed_two = (hat_two * norm2_gain).astype(jnp.bfloat16)
        logits = jnp.dot(normed_two, w_router, preferred_element_type=jnp.float32)
        choose = (route_rows[:, :, None] == expert_ids[None, None, :]).astype(jnp.float32)
        selected = jnp.einsum('re,rke->rk', logits, choose, precision=HIGH)
        raised = jnp.exp(selected)
        gates = raised / lax.optimization_barrier(jnp.sum(raised, axis=-1, keepdims=True))
        slot, slot_pair = slot_tables(route_rows, EXPERTS, CAP)
        padded = jnp.concatenate([normed_two, jnp.zeros((1, MODEL_WIDTH), jnp.bfloat16)], axis=0)
        sent = padded[slot_pair // TOPK].reshape(EXPERTS, CAP, MODEL_WIDTH)
        sent_float = sent.astype(jnp.float32)
        gate_act = jnp.einsum('ecd,edf->ecf', sent_float, gate_float)
        up_act = jnp.einsum('ecd,edf->ecf', sent_float, up_float)
        middle = (jax.nn.silu(gate_act) * up_act).astype(jnp.bfloat16)
        expert_out = jnp.einsum('ecf,efd->ecd', middle.astype(jnp.float32), down_float).astype(jnp.bfloat16)
        pair_out = expert_out.reshape(EXPERTS * CAP, MODEL_WIDTH)[slot].reshape(ROWS, TOPK, MODEL_WIDTH).astype(jnp.float32)
        mixed = jnp.einsum('rk,rkd->rd', gates, pair_out, precision=HIGH)
        out_rows = (hidden_rows + mixed).astype(jnp.bfloat16)
        cot_float = cot_rows.astype(jnp.float32)
        pair_cot = (gates[:, :, None] * cot_float[:, None, :]).astype(jnp.bfloat16).reshape(ROWS * TOPK, MODEL_WIDTH)
        grad_sent = jnp.concatenate([pair_cot, jnp.zeros((1, MODEL_WIDTH), jnp.bfloat16)], axis=0)[slot_pair].reshape(EXPERTS, CAP, MODEL_WIDTH)
        grad_float = grad_sent.astype(jnp.float32)
        d_gates = jnp.einsum('rd,rkd->rk', cot_float, pair_out, precision=HIGH)
        d_selected = gates * (d_gates - lax.optimization_barrier(jnp.sum(gates * d_gates, axis=-1, keepdims=True)))
        d_logits = jnp.einsum('rk,rke->re', d_selected, choose, precision=HIGH).astype(jnp.bfloat16)
        grad_router = grad_router + contract_first(normed_two, d_logits)
        grad_down = grad_down + jnp.einsum('ecf,ecd->efd', middle.astype(jnp.float32), grad_float)
        d_middle = jnp.einsum('ecd,efd->ecf', grad_float, down_float)
        sigmoid_gate = jax.nn.sigmoid(gate_act)
        d_gate_act = (d_middle * up_act * sigmoid_gate * (1.0 + gate_act * (1.0 - sigmoid_gate))).astype(jnp.bfloat16)
        d_up_act = (d_middle * jax.nn.silu(gate_act)).astype(jnp.bfloat16)
        grad_gate = grad_gate + jnp.einsum('ecd,ecf->edf', sent_float, d_gate_act.astype(jnp.float32))
        grad_up = grad_up + jnp.einsum('ecd,ecf->edf', sent_float, d_up_act.astype(jnp.float32))
        d_tokens = (jnp.einsum('ecf,edf->ecd', d_gate_act.astype(jnp.float32), gate_float) + jnp.einsum('ecf,edf->ecd', d_up_act.astype(jnp.float32), up_float)).astype(jnp.bfloat16)
        d_pairs = d_tokens.reshape(EXPERTS * CAP, MODEL_WIDTH)[slot].reshape(ROWS, TOPK, MODEL_WIDTH).astype(jnp.float32)
        d_normed_two = lax.optimization_barrier(jnp.sum(d_pairs, axis=1)) + contract_last(d_logits, w_router)
        grad_norm2 = grad_norm2 + lax.optimization_barrier(jnp.sum(d_normed_two * hat_two, axis=0))
        d_hidden = cot_float + normalize_back(d_normed_two, hat_two, inverse_two, norm2_gain)
        return ((grad_norm2, grad_router, grad_gate, grad_up, grad_down), (out_rows, d_hidden))
    block_count = TOKENS // ROWS
    start_moe = (jnp.zeros((MODEL_WIDTH,), jnp.float32), jnp.zeros((MODEL_WIDTH, EXPERTS), jnp.float32), jnp.zeros((EXPERTS, MODEL_WIDTH, FFE), jnp.float32), jnp.zeros((EXPERTS, MODEL_WIDTH, FFE), jnp.float32), jnp.zeros((EXPERTS, FFE, MODEL_WIDTH), jnp.float32))
    moe_carry, (out_blocks, d_hidden_blocks) = lax.scan(moe_block, start_moe, (hidden_all.reshape(block_count, ROWS, MODEL_WIDTH), routes.reshape(block_count, ROWS, TOPK), cotangent.reshape(block_count, ROWS, MODEL_WIDTH)))
    grad_norm2, grad_router, grad_gate, grad_up, grad_down = moe_carry

    def attention_back(carry, inputs):
        grad_norm1, grad_query, grad_key, grad_value, grad_out = carry
        seq_rows, seq_dh = inputs
        pieces = attention_pieces(seq_rows, norm1_gain, w_query, key_matrix, value_matrix, w_out, cosine_table, sine_table)
        hat_one, inverse_one, first_normed_input, query_rows, key_rows, value_rows, probs, probs_low, heads_flat, hidden = pieces
        d_attn = seq_dh.astype(jnp.bfloat16)
        grad_out = grad_out + contract_first(heads_flat, d_attn)
        head_gradient = contract_last(d_attn, w_out).astype(jnp.bfloat16)
        head_gradient = head_gradient.reshape(SEQUENCE_TOKENS, KEY_VALUE_HEADS, query_groups, HEAD_SIZE).transpose(1, 2, 0, 3).astype(jnp.float32)
        value_gradient = jnp.einsum('kgqv,kgqd->kvd', probs_low.astype(jnp.float32), head_gradient)
        d_probs = jnp.einsum('kgqd,kvd->kgqv', head_gradient, value_rows.astype(jnp.float32))
        d_scores = (probs * (d_probs - lax.optimization_barrier(jnp.sum(probs * d_probs, axis=-1, keepdims=True))) * scale).astype(jnp.bfloat16)
        d_queries = jnp.einsum('kgqv,kvd->kgqd', d_scores.astype(jnp.float32), key_rows.astype(jnp.float32))
        key_gradient = jnp.einsum('kgqv,kgqd->kvd', d_scores.astype(jnp.float32), query_rows.astype(jnp.float32))
        d_queries = unrotate_pairs(d_queries, cosine_table, sine_table).astype(jnp.bfloat16).transpose(2, 0, 1, 3).reshape(SEQUENCE_TOKENS, QUERY_HEADS * HEAD_SIZE)
        key_gradient = unrotate_pairs(key_gradient, cosine_table, sine_table).astype(jnp.bfloat16).transpose(1, 0, 2).reshape(SEQUENCE_TOKENS, KEY_VALUE_HEADS * HEAD_SIZE)
        value_gradient = value_gradient.astype(jnp.bfloat16).transpose(1, 0, 2).reshape(SEQUENCE_TOKENS, KEY_VALUE_HEADS * HEAD_SIZE)
        grad_query = grad_query + contract_first(first_normed_input, d_queries)
        grad_key = grad_key + contract_first(first_normed_input, key_gradient)
        grad_value = grad_value + contract_first(first_normed_input, value_gradient)
        d_normed_one = contract_last(d_queries, w_query) + contract_last(key_gradient, key_matrix) + contract_last(value_gradient, value_matrix)
        grad_norm1 = grad_norm1 + lax.optimization_barrier(jnp.sum(d_normed_one * hat_one, axis=0))
        d_rows = seq_dh + normalize_back(d_normed_one, hat_one, inverse_one, norm1_gain)
        return ((grad_norm1, grad_query, grad_key, grad_value, grad_out), d_rows)
    attention_begin = (jnp.zeros((MODEL_WIDTH,), jnp.float32), jnp.zeros((MODEL_WIDTH, QUERY_HEADS * HEAD_SIZE), jnp.float32), jnp.zeros((MODEL_WIDTH, KEY_VALUE_HEADS * HEAD_SIZE), jnp.float32), jnp.zeros((MODEL_WIDTH, KEY_VALUE_HEADS * HEAD_SIZE), jnp.float32), jnp.zeros((QUERY_HEADS * HEAD_SIZE, MODEL_WIDTH), jnp.float32))
    att_carry, d_rows_all = lax.scan(attention_back, attention_begin, (seq_input, d_hidden_blocks.reshape(seq_count, SEQUENCE_TOKENS, MODEL_WIDTH)))
    grad_norm1, grad_query, grad_key, grad_value, grad_out = att_carry
    return (out_blocks.reshape(TOKENS, MODEL_WIDTH), d_rows_all.reshape(TOKENS, MODEL_WIDTH), grad_norm1, grad_query, grad_key, grad_value, grad_out, grad_norm2, grad_router, grad_gate, grad_up, grad_down)
```

```python
import functools
import math

import jax
import jax.numpy as jnp
from jax import lax
from jax.sharding import PartitionSpec as P

QUERY_HEADS = 24
KEY_VALUE_HEADS = 8
HEAD_SIZE = 64
TOPK = 8
SEQUENCE_TOKENS = 512


EPS = 1e-06
THETA = 10000.0
HIGH = lax.Precision.HIGHEST


def rope_tables():
    half_size = HEAD_SIZE // 2
    freqs = jnp.exp(-jnp.log(THETA) * (2.0 * jnp.arange(half_size, dtype=jnp.float32)) / HEAD_SIZE)
    angles = jnp.arange(SEQUENCE_TOKENS, dtype=jnp.float32)[:, None] * freqs[None, :]
    return (jnp.cos(angles), jnp.sin(angles))


def rotate(tensor, cosine_table, sine_table):
    half_size = tensor.shape[-1] // 2
    first = tensor[..., :half_size]
    second = tensor[..., half_size:]
    return jnp.concatenate(
        [first * cosine_table - second * sine_table, second * cosine_table + first * sine_table],
        axis=-1,
    )


def unrotate_pairs(tensor, cosine_table, sine_table):
    half_size = tensor.shape[-1] // 2
    first = tensor[..., :half_size]
    second = tensor[..., half_size:]
    return jnp.concatenate(
        [first * cosine_table + second * sine_table, second * cosine_table - first * sine_table],
        axis=-1,
    )


def normalize(row_data):
    inverse = lax.rsqrt(jnp.mean(row_data * row_data, axis=-1, keepdims=True) + EPS)
    return (row_data * inverse, inverse)


def normalize_back(d_normed, normal_hat, inverse, gain):
    d_hat = d_normed * gain
    return inverse * (d_hat - normal_hat * jnp.mean(d_hat * normal_hat, axis=-1, keepdims=True))


def contract_first(left, right):
    return lax.dot_general(
        left, right, (((0,), (0,)), ((), ())), preferred_element_type=jnp.float32
    )


def contract_last(left, right):
    return lax.dot_general(
        left, right, (((1,), (1,)), ((), ())), preferred_element_type=jnp.float32
    )


def send(value, axis, pairs):
    return lax.ppermute(value, axis, pairs)


def line_gather(value, axis, size):
    mine = lax.axis_index(axis)
    upward = [value]
    downward = [value]
    for step in range(1, size):
        upward.append(send(upward[-1], axis, [(i, i + 1) for i in range(step - 1, size - 1)]))
        downward.append(send(downward[-1], axis, [(i, i - 1) for i in range(1, size - step + 1)]))
    blocks = [value]
    for k in range(1, size):
        blocks.append(jnp.where(mine + k < size, downward[k], upward[size - k]))
    return blocks


def line_scatter(blocks, axis, size):
    total = blocks[0].astype(jnp.float32)
    for sign in (1, -1):
        arrived = None
        for left in range(size - 1, 0, -1):
            part = blocks[left if sign > 0 else size - left]
            if arrived is not None:
                part = (part.astype(jnp.float32) + arrived.astype(jnp.float32)).astype(part.dtype)
            if sign > 0:
                pairs = [(i, i + 1) for i in range(size - left)]
            else:
                pairs = [(i, i - 1) for i in range(left, size)]
            arrived = send(part, axis, pairs)
        total = total + arrived.astype(jnp.float32)
    return total


class Tensor:
    def __init__(self, size):
        self.size = size
        self.halves = size // 2
        self.mine = lax.axis_index("tensor")
        self.half = self.mine // 2
        self.core = self.mine % 2

    def swap_core(self, value):
        return send(value, "tensor", [(t, t ^ 1) for t in range(self.size)])

    def shift_half(self, value, step):
        n = self.halves
        return send(
            value, "tensor", [(t, (t // 2 + step) % n * 2 + t % 2) for t in range(self.size)]
        )

    def gather(self, value):
        n = self.halves
        pieces = [value] + [self.shift_half(value, step) for step in range(1, n)]
        others = [self.swap_core(piece) for piece in pieces]
        out = jnp.zeros((n, 2) + value.shape, value.dtype)
        for step in range(n):
            where = (self.half - step) % n
            rest = (0,) * value.ndim
            out = lax.dynamic_update_slice(out, pieces[step][None, None], (where, self.core) + rest)
            out = lax.dynamic_update_slice(
                out, others[step][None, None], (where, 1 - self.core) + rest
            )
        return out.reshape((self.size,) + value.shape)

    def scatter(self, stacked):
        n = self.halves
        view = stacked.reshape((n, 2) + stacked.shape[1:])
        kept = lax.dynamic_index_in_dim(view, self.core, 1, keepdims=False)
        given = lax.dynamic_index_in_dim(view, 1 - self.core, 1, keepdims=False)
        pair = kept.astype(jnp.float32) + self.swap_core(given).astype(jnp.float32)
        total = lax.dynamic_index_in_dim(pair, self.half, 0, keepdims=False)
        for step in range(1, n):
            part = lax.dynamic_index_in_dim(pair, (self.half + step) % n, 0, keepdims=False)
            total = total + self.shift_half(part.astype(jnp.bfloat16), step).astype(jnp.float32)
        return total


def swap_all(value, sizes):
    for axis, size in sizes:
        bit = 1
        while bit < size:
            value = value + send(value, axis, [(i, i ^ bit) for i in range(size)])
            bit *= 2
    return value


def line_sum(value, sizes):
    size = sizes["expert"]
    mine = lax.axis_index("expert")
    rows = value.shape[0] // size
    blocks = [
        lax.dynamic_slice_in_dim(value, (mine + k) % size * rows, rows, 0) for k in range(size)
    ]
    part = line_scatter(blocks, "expert", size).astype(jnp.bfloat16)
    bit = 1
    while bit < sizes["dp"]:
        other = send(part, "dp", [(i, i ^ bit) for i in range(sizes["dp"])])
        part = (part.astype(jnp.float32) + other.astype(jnp.float32)).astype(jnp.bfloat16)
        bit *= 2
    out = jnp.zeros_like(value)
    for k, block in enumerate(line_gather(part, "expert", size)):
        out = lax.dynamic_update_slice_in_dim(out, block, (mine + k) % size * rows, 0)
    return out


def local(
    sizes,
    layer_input,
    norm1_gain,
    w_query,
    key_matrix,
    value_matrix,
    w_out,
    norm2_gain,
    w_router,
    w_gate,
    w_up,
    w_down,
    routes,
    cotangent,
):
    row_count, width = layer_input.shape
    expert_total = w_router.shape[1]
    owned = w_gate.shape[0]
    owners = sizes["expert"]
    everyone = [(axis, sizes[axis]) for axis in ("tensor", "expert", "dp")]
    place = lax.axis_index("expert")
    ring = Tensor(sizes["tensor"])
    query_width = w_query.shape[1]
    kv_width = key_matrix.shape[1]
    kv_local = kv_width // HEAD_SIZE
    query_groups = QUERY_HEADS // KEY_VALUE_HEADS
    scale = 1.0 / math.sqrt(HEAD_SIZE)
    cosine_table, sine_table = rope_tables()
    row_float = layer_input.astype(jnp.float32)
    hat_one, inverse_one = normalize(row_float)
    first_normed_input = (hat_one * norm1_gain).astype(jnp.bfloat16)
    normed_all = ring.gather(first_normed_input).reshape(-1, width)
    group_rows = normed_all.shape[0]
    seq_count = group_rows // SEQUENCE_TOKENS
    w_joined = jnp.concatenate([w_query, key_matrix, value_matrix], axis=1)
    projected = jnp.dot(normed_all, w_joined, preferred_element_type=jnp.float32)
    query_rows = (
        projected[:, :query_width]
        .reshape(seq_count, SEQUENCE_TOKENS, kv_local, query_groups, HEAD_SIZE)
        .transpose(0, 2, 3, 1, 4)
    )
    key_rows = (
        projected[:, query_width : query_width + kv_width]
        .reshape(seq_count, SEQUENCE_TOKENS, kv_local, HEAD_SIZE)
        .transpose(0, 2, 1, 3)
    )
    value_rows = (
        projected[:, query_width + kv_width :]
        .reshape(seq_count, SEQUENCE_TOKENS, kv_local, HEAD_SIZE)
        .transpose(0, 2, 1, 3)
    )
    value_rows = value_rows.astype(jnp.bfloat16)
    query_rows = rotate(query_rows, cosine_table, sine_table).astype(jnp.bfloat16)
    key_rows = rotate(key_rows, cosine_table, sine_table).astype(jnp.bfloat16)
    positions = jnp.arange(SEQUENCE_TOKENS, dtype=jnp.int32)
    causal = positions[:, None] >= positions[None, :]
    scores = (
        jnp.einsum("skgqd,skvd->skgqv", query_rows, key_rows, preferred_element_type=jnp.float32)
        * scale
    )
    log_total = jnp.log(jnp.sum(jnp.where(causal, jnp.exp(scores), 0.0), axis=-1, keepdims=True))
    probs = jnp.where(causal, jnp.exp(scores - log_total), 0.0)
    heads = jnp.einsum(
        "skgqv,skvd->skgqd",
        probs.astype(jnp.bfloat16),
        value_rows,
        preferred_element_type=jnp.float32,
    )
    heads_flat = (
        heads.astype(jnp.bfloat16).transpose(0, 3, 1, 2, 4).reshape(group_rows, query_width)
    )
    attended = ring.scatter(
        jnp.dot(heads_flat, w_out, preferred_element_type=jnp.float32).reshape(
            ring.size, row_count, width
        )
    )
    hidden = row_float + attended
    hat_two, inverse_two = normalize(hidden)
    normed_two = (hat_two * norm2_gain).astype(jnp.bfloat16)
    gate_all = ring.gather(w_gate).transpose(1, 0, 2, 3).reshape(owned, width, -1)
    up_all = ring.gather(w_up).transpose(1, 0, 2, 3).reshape(owned, width, -1)
    down_all = ring.gather(w_down).transpose(1, 0, 2, 3).reshape(owned, -1, width)
    tokens = jnp.concatenate(line_gather(normed_two, "expert", owners), axis=0)
    cots = jnp.concatenate(line_gather(cotangent, "expert", owners), axis=0)
    named = jnp.sum(
        (routes[:, :, None] == jnp.arange(expert_total, dtype=jnp.int32)).astype(jnp.bfloat16),
        axis=1,
    )
    named_all = jnp.concatenate(line_gather(named, "expert", owners), axis=0)
    raised = jnp.where(
        named_all > 0.5, jnp.exp(jnp.dot(tokens, w_router, preferred_element_type=jnp.float32)), 0.0
    )
    gates_all = raised / jnp.sum(raised, axis=-1, keepdims=True)
    gates = gates_all[:row_count]
    own_gates = lax.dynamic_slice_in_dim(gates_all, place * owned, owned, 1).T[:, :, None]
    gate_act = jnp.einsum("td,edf->etf", tokens, gate_all, preferred_element_type=jnp.float32)
    up_act = jnp.einsum("td,edf->etf", tokens, up_all, preferred_element_type=jnp.float32)
    sigmoid_gate = jax.nn.sigmoid(gate_act)
    silu_gate = gate_act * sigmoid_gate
    middle = silu_gate * up_act
    gated = (middle * own_gates).astype(jnp.bfloat16)
    moe = jnp.einsum("etf,efd->td", gated, down_all, preferred_element_type=jnp.float32)
    d_plain = jnp.einsum("td,efd->etf", cots, down_all, preferred_element_type=jnp.float32)
    d_gates = jnp.sum(d_plain * middle, axis=-1)
    d_middle = d_plain * own_gates
    d_gate_act = (
        d_middle * up_act * sigmoid_gate * (1.0 + gate_act * (1.0 - sigmoid_gate))
    ).astype(jnp.bfloat16)
    d_up_act = (d_middle * silu_gate).astype(jnp.bfloat16)
    d_tokens = jnp.einsum(
        "etf,edf->td", d_gate_act, gate_all, preferred_element_type=jnp.float32
    ) + jnp.einsum("etf,edf->td", d_up_act, up_all, preferred_element_type=jnp.float32)
    moe_blocks = moe.astype(jnp.bfloat16).reshape(owners, row_count, width)
    mixed = line_scatter([moe_blocks[k] for k in range(owners)], "expert", owners)
    layer_output = (hidden + mixed).astype(jnp.bfloat16)
    d_blocks = d_tokens.astype(jnp.bfloat16).reshape(owners, row_count, width)
    d_normed_two = line_scatter([d_blocks[k] for k in range(owners)], "expert", owners)
    d_gates = d_gates.reshape(owned, owners, row_count)
    d_gates_all = jnp.zeros((owners, owned, row_count), jnp.float32)
    for k in range(owners):
        part = d_gates[:, k]
        if k > 0:
            part = send(part, "expert", [(i, (i + k) % owners) for i in range(owners)])
        d_gates_all = lax.dynamic_update_slice(
            d_gates_all, part[None], ((place - k) % owners, 0, 0)
        )
    d_gates_all = d_gates_all.reshape(expert_total, row_count).T
    cot_float = cotangent.astype(jnp.float32)
    d_logits = (
        gates * (d_gates_all - jnp.sum(gates * d_gates_all, axis=-1, keepdims=True))
    ).astype(jnp.bfloat16)
    grad_router = contract_first(d_logits, normed_two)
    d_normed_two = d_normed_two + contract_last(d_logits, w_router)
    grad_gate = jnp.einsum("td,etf->edf", tokens, d_gate_act, preferred_element_type=jnp.float32)
    grad_up = jnp.einsum("td,etf->edf", tokens, d_up_act, preferred_element_type=jnp.float32)
    grad_down = jnp.einsum("etf,td->efd", gated, cots, preferred_element_type=jnp.float32)
    grad_norm2 = jnp.sum(d_normed_two * hat_two, axis=0)
    d_hidden = cot_float + normalize_back(d_normed_two, hat_two, inverse_two, norm2_gain)
    d_attn = d_hidden.astype(jnp.bfloat16)
    d_attn_all = ring.gather(d_attn).reshape(-1, width)
    grad_out = contract_first(heads_flat, d_attn_all)
    head_gradient = contract_last(d_attn_all, w_out).astype(jnp.bfloat16)
    head_gradient = head_gradient.reshape(
        seq_count, SEQUENCE_TOKENS, kv_local, query_groups, HEAD_SIZE
    ).transpose(0, 2, 3, 1, 4)
    again = (
        jnp.einsum("skgqd,skvd->skgqv", query_rows, key_rows, preferred_element_type=jnp.float32)
        * scale
    )
    probs = jnp.where(causal, jnp.exp(again - log_total), 0.0)
    value_gradient = jnp.einsum(
        "skgqv,skgqd->skvd",
        probs.astype(jnp.bfloat16),
        head_gradient,
        preferred_element_type=jnp.float32,
    )
    d_probs = jnp.einsum(
        "skgqd,skvd->skgqv", head_gradient, value_rows, preferred_element_type=jnp.float32
    )
    d_scores = (
        probs * (d_probs - jnp.sum(probs * d_probs, axis=-1, keepdims=True)) * scale
    ).astype(jnp.bfloat16)
    d_queries = jnp.einsum(
        "skgqv,skvd->skgqd", d_scores, key_rows, preferred_element_type=jnp.float32
    )
    key_gradient = jnp.einsum(
        "skgqv,skgqd->skvd", d_scores, query_rows, preferred_element_type=jnp.float32
    )
    d_queries = (
        unrotate_pairs(d_queries, cosine_table, sine_table)
        .astype(jnp.bfloat16)
        .transpose(0, 3, 1, 2, 4)
        .reshape(group_rows, query_width)
    )
    key_gradient = (
        unrotate_pairs(key_gradient, cosine_table, sine_table)
        .astype(jnp.bfloat16)
        .transpose(0, 2, 1, 3)
        .reshape(group_rows, kv_width)
    )
    value_gradient = (
        value_gradient.astype(jnp.bfloat16).transpose(0, 2, 1, 3).reshape(group_rows, kv_width)
    )
    d_projected = jnp.concatenate([d_queries, key_gradient, value_gradient], axis=1)
    grad_joined = contract_first(normed_all, d_projected)
    d_normed_one = ring.scatter(
        contract_last(d_projected, w_joined).reshape(ring.size, row_count, width)
    )
    grad_norm1 = jnp.sum(d_normed_one * hat_one, axis=0)
    d_input = d_hidden + normalize_back(d_normed_one, hat_one, inverse_one, norm1_gain)
    grad_joined = line_sum(grad_joined.astype(jnp.bfloat16), sizes).astype(jnp.float32)
    grad_query = grad_joined[:, :query_width]
    grad_key = grad_joined[:, query_width : query_width + kv_width]
    grad_value = grad_joined[:, query_width + kv_width :]
    grad_out = line_sum(grad_out.astype(jnp.bfloat16), sizes).astype(jnp.float32)
    small = jnp.concatenate([grad_router, grad_norm2[None], grad_norm1[None]], axis=0)
    small = swap_all(small, everyone)
    grad_router = small[:expert_total].T
    grad_norm2 = small[expert_total]
    grad_norm1 = small[expert_total + 1]

    def expert_sum(grad):
        rows = grad.shape[1] // ring.size
        parts = grad.astype(jnp.bfloat16).reshape(owned, ring.size, rows, grad.shape[2])
        total = ring.scatter(parts.transpose(1, 0, 2, 3)).astype(jnp.bfloat16)
        return swap_all(total, [("dp", sizes["dp"])]).astype(jnp.float32)

    grad_gate, grad_up, grad_down = expert_sum(grad_gate), expert_sum(grad_up), expert_sum(grad_down)
    return (
        layer_output,
        d_input,
        grad_norm1,
        grad_query,
        grad_key,
        grad_value,
        grad_out,
        grad_norm2,
        grad_router,
        grad_gate,
        grad_up,
        grad_down,
    )


def solution(mesh):
    in_specs = (
        P(("dp", "expert", "tensor"), None),
        P(),
        P(None, "tensor"),
        P(None, "tensor"),
        P(None, "tensor"),
        P("tensor", None),
        P(),
        P(),
        P("expert", "tensor", None),
        P("expert", "tensor", None),
        P("expert", "tensor", None),
        P(("dp", "expert", "tensor"), None),
        P(("dp", "expert", "tensor"), None),
    )
    out_specs = (
        P(("dp", "expert", "tensor"), None),
        P(("dp", "expert", "tensor"), None),
        P(),
        P(None, "tensor"),
        P(None, "tensor"),
        P(None, "tensor"),
        P("tensor", None),
        P(),
        P(),
        P("expert", "tensor", None),
        P("expert", "tensor", None),
        P("expert", "tensor", None),
    )
    return jax.shard_map(
        functools.partial(local, dict(mesh.shape)), mesh=mesh, in_specs=in_specs, out_specs=out_specs, check_vma=False)
```

```python
import functools
import math

import jax
import jax.numpy as jnp
from jax import lax
from jax.experimental import pallas as pl
from jax.experimental.pallas import tpu as pltpu
from jax.sharding import PartitionSpec as P

QUERY_HEADS = 24
KEY_VALUE_HEADS = 8
HEAD_SIZE = 64
TOPK = 8
SEQUENCE_TOKENS = 512
LANES = 128
TILE = 256

EPS = 1e-06
THETA = 10000.0
SCALE = 1.0 / math.sqrt(HEAD_SIZE)
GROUP = QUERY_HEADS // KEY_VALUE_HEADS
BF16 = jnp.bfloat16
F32 = jnp.float32


def dot(left, right):
    return jnp.dot(left, right, preferred_element_type=F32)


def contract_first(left, right):
    return lax.dot_general(left, right, (((0,), (0,)), ((), ())), preferred_element_type=F32)


def contract_last(left, right):
    return lax.dot_general(left, right, (((1,), (1,)), ((), ())), preferred_element_type=F32)


def rope_tables():
    half_size = HEAD_SIZE // 2
    freqs = jnp.exp(-jnp.log(THETA) * (2.0 * jnp.arange(half_size, dtype=F32)) / HEAD_SIZE)
    angles = jnp.arange(SEQUENCE_TOKENS, dtype=F32)[:, None] * freqs[None, :]
    return (jnp.cos(angles), jnp.sin(angles))


def lane_tables():
    cosine, sine = rope_tables()
    return jnp.tile(cosine, (1, 4)), jnp.tile(jnp.concatenate([-sine, sine], axis=1), (1, 2))


def lane_index(shape):
    return lax.broadcasted_iota(jnp.int32, shape, len(shape) - 1)


def swapped(tile):
    half = HEAD_SIZE // 2
    low = lane_index(tile.shape) % HEAD_SIZE < half
    return jnp.where(low, pltpu.roll(tile, LANES - half, 1), pltpu.roll(tile, half, 1))


def spread(tile):
    low = lane_index(tile.shape) < HEAD_SIZE
    moved = pltpu.roll(tile, HEAD_SIZE, 1)
    zero = jnp.zeros_like(tile)
    return [
        jnp.where(low, tile, zero),
        jnp.where(low, zero, moved),
        jnp.where(low, moved, zero),
        jnp.where(low, zero, tile),
    ]


def gathered(spreads):
    return (
        spreads[0]
        + pltpu.roll(spreads[1], HEAD_SIZE, 1)
        + pltpu.roll(spreads[2], HEAD_SIZE, 1)
        + spreads[3]
    )


def causal_mask(shape, key_dim):
    keys = lax.broadcasted_iota(jnp.int32, shape, key_dim)
    queries = lax.broadcasted_iota(jnp.int32, shape, 1 - key_dim)
    return keys <= queries + (shape[key_dim] - shape[1 - key_dim])


def attention_forward_kernel(
    core_ref, near_ref, far_ref, joined_ref, out_ref, first_ref, second_ref,
    kept_ref, given_ref, rows_ref, query_ref, key_ref, value_ref, heads_ref,
    key_spread, value_spread,
):
    core = core_ref[0]
    block = near_ref.shape[0]
    query_width = query_ref.shape[1]
    own = pl.ds(pl.multiple_of(core * block, block), block)
    other = pl.ds(pl.multiple_of((1 - core) * block, block), block)
    rows_ref[own, :] = near_ref[...]
    rows_ref[other, :] = far_ref[...]
    projected = dot(rows_ref[...], joined_ref[...])
    first, second = first_ref[...], second_ref[...]
    for j in range(query_width // LANES):
        tile = projected[:, j * LANES : (j + 1) * LANES]
        query_ref[:, j * LANES : (j + 1) * LANES] = (tile * first + swapped(tile) * second).astype(BF16)
    tile = projected[:, query_width : query_width + LANES]
    key = (tile * first + swapped(tile) * second).astype(BF16)
    value = projected[:, query_width + LANES :].astype(BF16)
    key_ref[...] = key
    value_ref[...] = value
    for i, part in enumerate(spread(key.astype(F32))):
        key_spread[i] = part.astype(BF16)
    for i, part in enumerate(spread(value.astype(F32))):
        value_spread[i] = part.astype(BF16)

    def pair(j, carry):
        lanes = pl.ds(pl.multiple_of(j * LANES, LANES), LANES)
        for begin in range(0, rows_ref.shape[0], TILE):
            end = begin + TILE
            query = query_ref[begin:end, lanes]
            total = jnp.zeros((TILE, LANES), F32)
            for half in range(2):
                index = (2 * j + half) // GROUP * 2 + half
                scores = contract_last(query, key_spread[index, :end, :]) * SCALE
                mask = causal_mask(scores.shape, 1)
                sums = jnp.sum(jnp.where(mask, jnp.exp(scores), 0.0), axis=1, keepdims=True)
                probs = jnp.where(mask, jnp.exp(scores - jnp.log(sums)), 0.0).astype(BF16)
                total = total + dot(probs, value_spread[index, :end, :])
            heads_ref[begin:end, lanes] = total.astype(BF16)
        return carry

    lax.fori_loop(0, query_width // LANES, pair, 0)
    kept_ref[...] = dot(heads_ref[own, :], out_ref[...]).astype(BF16)
    given_ref[...] = dot(heads_ref[other, :], out_ref[...]).astype(BF16)


def vmem():
    return pl.BlockSpec(memory_space=pltpu.VMEM)


def attention_forward(core, near, far, joined, w_out, tables):
    block, width = near.shape
    rows = 2 * block
    query_width = w_out.shape[0]
    shapes = [
        (block, width), (block, width), (rows, width), (rows, query_width),
        (rows, LANES), (rows, LANES), (rows, query_width),
    ]
    flops = 2 * rows * (width * (joined.shape[1] + query_width) + 2 * rows * query_width)
    return pl.pallas_call(
        attention_forward_kernel,
        out_shape=[jax.ShapeDtypeStruct(shape, BF16) for shape in shapes],
        in_specs=[pl.BlockSpec(memory_space=pltpu.SMEM)] + [vmem() for _ in range(6)],
        out_specs=[vmem() for _ in shapes],
        scratch_shapes=[pltpu.VMEM((4, rows, LANES), BF16), pltpu.VMEM((4, rows, LANES), BF16)],
        compiler_params=pltpu.CompilerParams(vmem_limit_bytes=40 << 20),
        cost_estimate=pl.CostEstimate(flops=flops, bytes_accessed=12 << 20, transcendentals=1 << 22),
    )(core, near, far, joined, w_out, *tables)


def attention_backward_kernel(
    core_ref, near_ref, far_ref, joined_ref, out_ref, first_ref, second_ref,
    query_ref, key_ref, value_ref,
    kept_ref, given_ref, rows_ref, projected_ref,
    key_spread, value_spread, key_sum, value_sum, heads,
):
    core = core_ref[0]
    block = near_ref.shape[0]
    query_width = query_ref.shape[1]
    own = pl.ds(pl.multiple_of(core * block, block), block)
    other = pl.ds(pl.multiple_of((1 - core) * block, block), block)
    rows_ref[own, :] = near_ref[...]
    rows_ref[other, :] = far_ref[...]
    heads[...] = contract_last(rows_ref[...], out_ref[...]).astype(BF16)
    for i, part in enumerate(spread(key_ref[...].astype(F32))):
        key_spread[i] = part.astype(BF16)
    for i, part in enumerate(spread(value_ref[...].astype(F32))):
        value_spread[i] = part.astype(BF16)
    key_sum[...] = jnp.zeros_like(key_sum)
    value_sum[...] = jnp.zeros_like(value_sum)

    def pair(j, carry):
        lanes = pl.ds(pl.multiple_of(j * LANES, LANES), LANES)
        for begin in range(0, rows_ref.shape[0], TILE):
            end = begin + TILE
            query = query_ref[begin:end, lanes]
            grad = heads[begin:end, lanes]
            low = lane_index(query.shape) < HEAD_SIZE
            zero = jnp.zeros(query.shape, BF16)
            total = jnp.zeros((TILE, LANES), F32)
            for half in range(2):
                index = (2 * j + half) // GROUP * 2 + half
                key = key_spread[index, :end, :]
                scores = contract_last(key, query) * SCALE
                mask = causal_mask(scores.shape, 0)
                sums = jnp.sum(jnp.where(mask, jnp.exp(scores), 0.0), axis=0, keepdims=True)
                probs = jnp.where(mask, jnp.exp(scores - jnp.log(sums)), 0.0)
                d_probs = contract_last(value_spread[index, :end, :], grad)
                mean = jnp.sum(probs * d_probs, axis=0, keepdims=True)
                d_scores = (probs * (d_probs - mean) * SCALE).astype(BF16)
                mine = low if half == 0 else jnp.logical_not(low)
                value_sum[index, :end, :] += dot(probs.astype(BF16), jnp.where(mine, grad, zero))
                key_sum[index, :end, :] += dot(d_scores, jnp.where(mine, query, zero))
                total = total + contract_first(d_scores, key)
            first, second = first_ref[begin:end, :], second_ref[begin:end, :]
            projected_ref[begin:end, lanes] = (total * first - swapped(total) * second).astype(BF16)
        return carry

    lax.fori_loop(0, query_width // LANES, pair, 0)
    total = gathered([key_sum[i] for i in range(4)])
    projected_ref[:, query_width : query_width + LANES] = (
        total * first_ref[...] - swapped(total) * second_ref[...]
    ).astype(BF16)
    projected_ref[:, query_width + LANES :] = gathered([value_sum[i] for i in range(4)]).astype(BF16)
    kept_ref[...] = contract_last(projected_ref[own, :], joined_ref[...]).astype(BF16)
    given_ref[...] = contract_last(projected_ref[other, :], joined_ref[...]).astype(BF16)


def attention_backward(core, near, far, joined, w_out, tables, query, key, value):
    block, width = near.shape
    rows = 2 * block
    query_width = w_out.shape[0]
    shapes = [(block, width), (block, width), (rows, width), (rows, joined.shape[1])]
    flops = 2 * rows * (width * (joined.shape[1] + query_width) + 5 * rows * query_width)
    return pl.pallas_call(
        attention_backward_kernel,
        out_shape=[jax.ShapeDtypeStruct(shape, BF16) for shape in shapes],
        in_specs=[pl.BlockSpec(memory_space=pltpu.SMEM)] + [vmem() for _ in range(9)],
        out_specs=[vmem() for _ in shapes],
        scratch_shapes=[
            pltpu.VMEM((4, rows, LANES), BF16),
            pltpu.VMEM((4, rows, LANES), BF16),
            pltpu.VMEM((4, rows, LANES), F32),
            pltpu.VMEM((4, rows, LANES), F32),
            pltpu.VMEM((rows, query_width), BF16),
        ],
        compiler_params=pltpu.CompilerParams(vmem_limit_bytes=40 << 20),
        cost_estimate=pl.CostEstimate(flops=flops, bytes_accessed=12 << 20, transcendentals=1 << 22),
    )(core, near, far, joined, w_out, *tables, query, key, value)


def experts_kernel(
    place_ref, order_ref, tokens_ref, cots_ref, router_ref, gate_ref, up_ref, *refs, pieces
):
    down_refs, refs = refs[:pieces], refs[pieces:]
    (moe_ref, back_ref, gates_ref, gated_ref, d_gate_ref, d_up_ref,
     down, moe_sum, back_sum, d_gates) = refs
    expert, tile = pl.program_id(0), pl.program_id(1)
    width = tokens_ref.shape[1]
    rows = pl.ds(pl.multiple_of(tile * TILE, TILE), TILE)
    lane = place_ref[0] + expert

    @pl.when(tile == 0)
    def _():
        for piece in range(pieces):
            size = down_refs[piece].shape[1]
            at = pl.multiple_of(order_ref[piece] * size, size)
            down[pl.ds(at, size), :] = down_refs[piece][0]

    tokens = tokens_ref[rows, :]
    cots = cots_ref[rows, :width]

    @pl.when(expert == 0)
    def _():
        logits = dot(tokens, router_ref[...])
        raised = jnp.where(cots_ref[rows, width:] > 0.5, jnp.exp(logits), 0.0)
        gates_ref[rows, :] = raised / jnp.sum(raised, axis=1, keepdims=True)
        d_gates[rows, :] = jnp.zeros((TILE, LANES), F32)
        moe_sum[rows, :] = jnp.zeros((TILE, width), F32)
        back_sum[rows, :] = jnp.zeros((TILE, width), F32)

    chosen = lane_index((TILE, LANES)) == lane
    gates = jnp.sum(jnp.where(chosen, gates_ref[rows, :], 0.0), axis=1, keepdims=True)
    gate_act = dot(tokens, gate_ref[0])
    up_act = dot(tokens, up_ref[0])
    sigmoid = jax.nn.sigmoid(gate_act)
    silu = gate_act * sigmoid
    middle = silu * up_act
    gated = (gates * middle).astype(BF16)
    gated_ref[0] = gated
    moe_sum[rows, :] += dot(gated, down[...])
    plain = contract_last(cots, down[...])
    d_gate = jnp.sum(plain * middle, axis=1, keepdims=True)
    d_gates[rows, :] += jnp.where(chosen, d_gate, 0.0)
    d_middle = plain * gates
    d_gate_act = (d_middle * up_act * sigmoid * (1.0 + gate_act * (1.0 - sigmoid))).astype(BF16)
    d_up_act = (d_middle * silu).astype(BF16)
    d_gate_ref[0] = d_gate_act
    d_up_ref[0] = d_up_act
    back_sum[rows, :] += contract_last(d_gate_act, gate_ref[0]) + contract_last(d_up_act, up_ref[0])

    @pl.when(expert == pl.num_programs(0) - 1)
    def _():
        moe_ref[rows, :] = moe_sum[rows, :].astype(BF16)
        back_ref[rows, :width] = back_sum[rows, :].astype(BF16)
        whole = d_gates[rows, :]
        high = whole.astype(BF16).astype(F32)
        back_ref[rows, width:] = (high + pltpu.roll(whole - high, LANES // 2, 1)).astype(BF16)


def experts(place, order, tokens, cots, router, w_gate, w_up, down_pieces):
    count, width = tokens.shape
    owned, _, hidden = w_gate.shape
    grid = (owned, count // TILE)

    def whole(shape):
        return pl.BlockSpec(shape, lambda e, t, *_: (0, 0))

    def expert(shape):
        return pl.BlockSpec((1,) + shape[1:], lambda e, t, *_: (e, 0, 0))

    rows_spec = pl.BlockSpec((1, TILE, hidden), lambda e, t, *_: (e, t, 0))
    products = jax.ShapeDtypeStruct((owned, count, hidden), BF16)
    return pl.pallas_call(
        functools.partial(experts_kernel, pieces=len(down_pieces)),
        out_shape=[
            jax.ShapeDtypeStruct((count, width), BF16),
            jax.ShapeDtypeStruct((count, width + LANES), BF16),
            jax.ShapeDtypeStruct((count, LANES), F32),
            products, products, products,
        ],
        grid_spec=pltpu.PrefetchScalarGridSpec(
            num_scalar_prefetch=2,
            grid=grid,
            in_specs=[
                whole(tokens.shape), whole(cots.shape), whole(router.shape),
                expert(w_gate.shape), expert(w_up.shape),
                *(expert(piece.shape) for piece in down_pieces),
            ],
            out_specs=[
                whole((count, width)), whole((count, width + LANES)), whole((count, LANES)),
                rows_spec, rows_spec, rows_spec,
            ],
            scratch_shapes=[
                pltpu.VMEM((hidden, width), BF16),
                pltpu.VMEM((count, width), F32),
                pltpu.VMEM((count, width), F32),
                pltpu.VMEM((count, LANES), F32),
            ],
        ),
        compiler_params=pltpu.CompilerParams(vmem_limit_bytes=56 << 20),
        cost_estimate=pl.CostEstimate(
            flops=12 * count * width * hidden * owned,
            bytes_accessed=6 * width * hidden * owned + 24 * count * width,
            transcendentals=count * hidden * owned,
        ),
    )(place, order, tokens, cots, router, w_gate, w_up, *down_pieces)


def rotate(tensor, cosine_table, sine_table):
    half_size = tensor.shape[-1] // 2
    first = tensor[..., :half_size]
    second = tensor[..., half_size:]
    return jnp.concatenate(
        [first * cosine_table - second * sine_table, second * cosine_table + first * sine_table],
        axis=-1,
    )


def plain_scores(query_rows, key_rows):
    scores = (
        jnp.einsum("skgqd,skvd->skgqv", query_rows, key_rows, preferred_element_type=F32) * SCALE
    )
    positions = jnp.arange(SEQUENCE_TOKENS, dtype=jnp.int32)
    causal = positions[:, None] >= positions[None, :]
    total = jnp.sum(jnp.where(causal, jnp.exp(scores), 0.0), axis=-1, keepdims=True)
    return jnp.where(causal, jnp.exp(scores - jnp.log(total)), 0.0)


def plain_forward(normed_all, joined, w_out):
    query_width = w_out.shape[0]
    kv_local = query_width // GROUP // HEAD_SIZE
    cosine_table, sine_table = rope_tables()
    projected = dot(normed_all, joined)
    split = (-1, SEQUENCE_TOKENS, kv_local)
    query = projected[:, :query_width].reshape(*split, GROUP, HEAD_SIZE).transpose(0, 2, 3, 1, 4)
    key, value = (
        part.reshape(*split, HEAD_SIZE).transpose(0, 2, 1, 3)
        for part in jnp.split(projected[:, query_width:], 2, axis=1)
    )
    value = value.astype(BF16)
    query = rotate(query, cosine_table, sine_table).astype(BF16)
    key = rotate(key, cosine_table, sine_table).astype(BF16)
    probs = plain_scores(query, key).astype(BF16)
    heads = jnp.einsum("skgqv,skvd->skgqd", probs, value, preferred_element_type=F32)
    heads = heads.astype(BF16).transpose(0, 3, 1, 2, 4).reshape(-1, query_width)
    return dot(heads, w_out), query, key, value, heads


def plain_backward(d_attn_all, joined, w_out, query, key, value):
    query_width = w_out.shape[0]
    rows = d_attn_all.shape[0]
    kv_local = query_width // GROUP // HEAD_SIZE
    cosine_table, sine_table = rope_tables()
    grad = contract_last(d_attn_all, w_out).astype(BF16)
    grad = grad.reshape(-1, SEQUENCE_TOKENS, kv_local, GROUP, HEAD_SIZE).transpose(0, 2, 3, 1, 4)
    probs = plain_scores(query, key)
    d_value = jnp.einsum(
        "skgqv,skgqd->skvd", probs.astype(BF16), grad, preferred_element_type=F32
    )
    d_probs = jnp.einsum("skgqd,skvd->skgqv", grad, value, preferred_element_type=F32)
    d_scores = (
        probs * (d_probs - jnp.sum(probs * d_probs, axis=-1, keepdims=True)) * SCALE
    ).astype(BF16)
    d_query = jnp.einsum("skgqv,skvd->skgqd", d_scores, key, preferred_element_type=F32)
    d_key = jnp.einsum("skgqv,skgqd->skvd", d_scores, query, preferred_element_type=F32)
    d_query = rotate(d_query, cosine_table, -sine_table).astype(BF16).transpose(0, 3, 1, 2, 4)
    d_key = rotate(d_key, cosine_table, -sine_table).astype(BF16).transpose(0, 2, 1, 3)
    d_value = d_value.astype(BF16).transpose(0, 2, 1, 3)
    return jnp.concatenate([part.reshape(rows, -1) for part in (d_query, d_key, d_value)], axis=1)


def normalize(row_data):
    inverse = lax.rsqrt(jnp.mean(row_data * row_data, axis=-1, keepdims=True) + EPS)
    return (row_data * inverse, inverse)


def normalize_back(d_normed, normal_hat, inverse, gain):
    d_hat = d_normed * gain
    return inverse * (d_hat - normal_hat * jnp.mean(d_hat * normal_hat, axis=-1, keepdims=True))


def send(value, axis, pairs):
    return lax.ppermute(value, axis, pairs)


def after(value, *earlier):
    return lax.optimization_barrier((value, *earlier))[0]


def add(*parts):
    return sum(part.astype(F32) for part in parts)


class Line:
    def __init__(self, size):
        self.size = size
        self.mine = lax.axis_index("expert")

    def fetch(self, value, distance):
        n = self.size
        return send(value, "expert", [((i + distance) % n, i) for i in range(n)])

    def deliver(self, value, distance):
        n = self.size
        return send(value, "expert", [(i, (i + distance) % n) for i in range(n)])


class Tensor:
    def __init__(self, size):
        self.size = size
        self.halves = size // 2
        self.mine = lax.axis_index("tensor")
        self.half = self.mine // 2
        self.core = self.mine % 2

    def swap_core(self, value):
        return send(value, "tensor", [(t, t ^ 1) for t in range(self.size)])

    def shift_half(self, value, step):
        n = self.halves
        return send(
            value, "tensor", [(t, (t // 2 + step) % n * 2 + t % 2) for t in range(self.size)]
        )

    def pieces(self, value):
        mine = [value] + [self.shift_half(value, step) for step in range(1, self.halves)]
        return [piece for one in mine for piece in (one, self.swap_core(one))]

    def order(self):
        places = []
        for step in range(self.halves):
            half = (self.half - step) % self.halves
            places += [half * 2 + self.core, half * 2 + 1 - self.core]
        return places

    def gather(self, value):
        out = jnp.zeros((self.size,) + value.shape, value.dtype)
        for place, piece in zip(self.order(), self.pieces(value)):
            out = lax.dynamic_update_slice(out, piece[None], (place,) + (0,) * value.ndim)
        return out

    def scatter(self, stacked):
        n = self.halves
        view = stacked.reshape((n, 2) + stacked.shape[1:])
        kept = lax.dynamic_index_in_dim(view, self.core, 1, keepdims=False)
        given = lax.dynamic_index_in_dim(view, 1 - self.core, 1, keepdims=False)
        pair = add(kept, self.swap_core(given))
        total = lax.dynamic_index_in_dim(pair, self.half, 0, keepdims=False)
        for step in range(1, n):
            part = lax.dynamic_index_in_dim(pair, (self.half + step) % n, 0, keepdims=False)
            total = add(total, self.shift_half(part.astype(BF16), step))
        return total


def swap_all(value, sizes):
    for axis, size in sizes:
        bit = 1
        while bit < size:
            value = value + send(value, axis, [(i, i ^ bit) for i in range(size)])
            bit *= 2
    return value


def local(
    sizes,
    layer_input,
    norm1_gain,
    w_query,
    key_matrix,
    value_matrix,
    w_out,
    norm2_gain,
    w_router,
    w_gate,
    w_up,
    w_down,
    routes,
    cotangent,
):
    row_count, width = layer_input.shape
    expert_total = w_router.shape[1]
    owned = w_gate.shape[0]
    ring = Tensor(sizes["tensor"])
    line = Line(sizes["expert"])
    query_width = w_query.shape[1]
    kv_width = key_matrix.shape[1]
    by_kernel = (
        2 * row_count == SEQUENCE_TOKENS and query_width % LANES == 0 and kv_width == LANES
    )
    core = ring.core.astype(jnp.int32)[None]
    joined = jnp.concatenate([w_query, key_matrix, value_matrix], axis=1)
    tables = lane_tables()

    row_float = layer_input.astype(F32)
    hat_one, inverse_one = normalize(row_float)
    normed_one = (hat_one * norm1_gain).astype(BF16)
    if by_kernel:
        partner = ring.swap_core(normed_one)
        across = ring.shift_half(normed_one, 1)
        near = attention_forward(core, normed_one, partner, joined, w_out, tables)
        far = attention_forward(core, across, ring.swap_core(across), joined, w_out, tables)
        far_sum = add(far[0], ring.swap_core(far[1])).astype(BF16)
        attended = add(near[0], ring.swap_core(near[1]), ring.shift_half(far_sum, 1))
    else:
        normed_all = ring.gather(normed_one).reshape(-1, width)
        attended, query, key, value, heads = plain_forward(normed_all, joined, w_out)
        attended = ring.scatter(attended.reshape(ring.size, row_count, width))
    hidden = row_float + attended

    hat_two, inverse_two = normalize(hidden)
    normed_two = (hat_two * norm2_gain).astype(BF16)
    gate_all = lax.all_gather(w_gate, "tensor", axis=1, tiled=True)
    up_all = lax.all_gather(w_up, "tensor", axis=1, tiled=True)
    down_pieces = ring.pieces(w_down)
    order = jnp.stack(ring.order()).astype(jnp.int32)
    named = jnp.sum(
        (routes[:, :, None] == jnp.arange(LANES, dtype=jnp.int32)).astype(BF16), axis=1
    )
    cots = jnp.concatenate([cotangent, named], axis=1)
    middle = line.size // 2
    early = list(range(0, line.size, middle))
    late = [k for k in range(line.size) if k % middle]
    cots_of = {k: line.fetch(cots, k) if k else cots for k in range(line.size)}
    tokens_of = {k: line.fetch(normed_two, k) if k else normed_two for k in early}
    held = after(normed_two, *(tokens_of[k] for k in early[1:]))
    tokens_of.update({k: line.fetch(held, k) for k in late})
    router = jnp.pad(w_router, ((0, 0), (0, LANES - expert_total)))
    place = (line.mine * owned).astype(jnp.int32)[None]

    moe_of, back_of, tokens, cotangents, products = {}, {}, [], [], []
    for group in (early, late):
        rows = jnp.concatenate([tokens_of[k] for k in group], axis=0)
        grads = jnp.concatenate([cots_of[k] for k in group], axis=0)
        moe, back, gates_group, *made = experts(
            place, order, rows, grads, router, gate_all, up_all, down_pieces
        )
        if 0 in group:
            gates = gates_group[:row_count]
        for i, k in enumerate(group):
            moe_of[k] = moe[i * row_count : (i + 1) * row_count]
            back_of[k] = back[i * row_count : (i + 1) * row_count]
        tokens.append(rows)
        cotangents.append(grads[:, :width])
        products.append(made)
    tokens = jnp.concatenate(tokens, axis=0)
    cotangents = jnp.concatenate(cotangents, axis=0)
    gated, d_gate_act, d_up_act = (
        jnp.concatenate([made[i] for made in products], axis=1) for i in range(3)
    )
    backs = [back_of[0]] + [line.deliver(back_of[k], k) for k in range(1, line.size)]
    back = add(*backs)
    d_normed_two = back[:, :width]
    d_gates = back[:, width : width + LANES // 2] + back[:, width + LANES // 2 :]
    moes = [moe_of[0]] + [
        line.deliver(after(moe_of[k], *backs), k) for k in range(1, line.size)
    ]
    layer_output = (hidden + add(*moes)).astype(BF16)

    gates = gates[:, : LANES // 2]
    d_logits = (gates * (d_gates - jnp.sum(gates * d_gates, axis=-1, keepdims=True))).astype(BF16)
    grad_router = contract_first(d_logits, normed_two)[:expert_total]
    d_normed_two = d_normed_two + contract_last(d_logits, router[:, : LANES // 2])
    grad_norm2 = jnp.sum(d_normed_two * hat_two, axis=0)
    d_hidden = cotangent.astype(F32) + normalize_back(
        d_normed_two, hat_two, inverse_two, norm2_gain
    )

    d_attn = d_hidden.astype(BF16)
    if by_kernel:
        d_partner = ring.swap_core(d_attn)
        d_across = ring.shift_half(d_attn, 1)
        near_back = attention_backward(
            core, d_attn, d_partner, joined, w_out, tables, *near[3:6]
        )
        far_back = attention_backward(
            core, d_across, ring.swap_core(d_across), joined, w_out, tables, *far[3:6]
        )
        far_sum = add(far_back[0], ring.swap_core(far_back[1])).astype(BF16)
        d_normed_one = add(
            near_back[0], ring.swap_core(near_back[1]), ring.shift_half(far_sum, 1)
        )
        grad_out = contract_first(near[6], near_back[2]) + contract_first(far[6], far_back[2])
        grad_joined = contract_first(near[2], near_back[3]) + contract_first(far[2], far_back[3])
    else:
        d_attn_all = ring.gather(d_attn).reshape(-1, width)
        d_projected = plain_backward(d_attn_all, joined, w_out, query, key, value)
        d_normed_one = ring.scatter(
            contract_last(d_projected, joined).reshape(ring.size, row_count, width)
        )
        grad_out = contract_first(heads, d_attn_all)
        grad_joined = contract_first(normed_all, d_projected)
    grad_norm1 = jnp.sum(d_normed_one * hat_one, axis=0)
    d_input = d_hidden + normalize_back(d_normed_one, hat_one, inverse_one, norm1_gain)

    grad_joined, grad_out = (
        grad.astype(F32)
        for grad in lax.psum((grad_joined.astype(BF16), grad_out.astype(BF16)), ("dp", "expert"))
    )
    grad_query = grad_joined[:, :query_width]
    grad_key = grad_joined[:, query_width : query_width + kv_width]
    grad_value = grad_joined[:, query_width + kv_width :]
    small = jnp.concatenate([grad_router, grad_norm2[None], grad_norm1[None]], axis=0)
    small = swap_all(small, [(axis, sizes[axis]) for axis in ("tensor", "expert", "dp")])

    def over_copies(grad):
        return swap_all(grad, [("dp", sizes["dp"])]).astype(F32)

    grad_down = jnp.einsum("etf,td->efd", gated, cotangents, preferred_element_type=F32)
    grad_down = lax.psum_scatter(
        grad_down.astype(BF16), "tensor", scatter_dimension=1, tiled=True
    )
    columns = [
        lax.dynamic_slice_in_dim(tokens, place * w_gate.shape[1], w_gate.shape[1], 1)
        for place in ring.order()
    ]
    grad_gate, grad_up = (
        own_share(ring, columns, product).astype(BF16) for product in (d_gate_act, d_up_act)
    )
    return (
        layer_output,
        d_input,
        small[expert_total + 1],
        grad_query,
        grad_key,
        grad_value,
        grad_out,
        small[expert_total],
        small[:expert_total].T,
        over_copies(grad_gate),
        over_copies(grad_up),
        over_copies(grad_down),
    )


def own_share(ring, columns, product):
    def grads(parts):
        return jnp.einsum(
            "td,etf->edf", jnp.concatenate(parts, axis=1), product, preferred_element_type=F32
        ).astype(BF16)

    rows = columns[0].shape[1]
    given = ring.swap_core(grads(columns[1::2]))
    pair = add(grads(columns[0::2]), given)
    total = pair[:, :rows]
    for step in range(1, ring.halves):
        part = pair[:, step * rows : (step + 1) * rows].astype(BF16)
        total = add(total, ring.shift_half(part, ring.halves - step))
    return total


def solution(mesh):
    in_specs = (
        P(("dp", "expert", "tensor"), None),
        P(),
        P(None, "tensor"),
        P(None, "tensor"),
        P(None, "tensor"),
        P("tensor", None),
        P(),
        P(),
        P("expert", "tensor", None),
        P("expert", "tensor", None),
        P("expert", "tensor", None),
        P(("dp", "expert", "tensor"), None),
        P(("dp", "expert", "tensor"), None),
    )
    out_specs = (
        P(("dp", "expert", "tensor"), None),
        P(("dp", "expert", "tensor"), None),
        P(),
        P(None, "tensor"),
        P(None, "tensor"),
        P(None, "tensor"),
        P("tensor", None),
        P(),
        P(),
        P("expert", "tensor", None),
        P("expert", "tensor", None),
        P("expert", "tensor", None),
    )
    return jax.shard_map(
        functools.partial(local, dict(mesh.shape)),
        mesh=mesh,
        in_specs=in_specs,
        out_specs=out_specs,
        check_vma=False,
    )
```

```python
import functools
import math

import jax
import jax.numpy as jnp
from jax import lax
from jax.experimental import pallas as pl
from jax.experimental.pallas import tpu as pltpu
from jax.sharding import PartitionSpec as P


QUERY_HEADS = 24
KEY_VALUE_HEADS = 8
HEAD_SIZE = 64
SEQUENCE_TOKENS = 512
LANES = 128
TILE = 256

EPS = 1e-06
THETA = 10000.0
SCALE = 1.0 / math.sqrt(HEAD_SIZE)
GROUP = QUERY_HEADS // KEY_VALUE_HEADS
BF16 = jnp.bfloat16
F32 = jnp.float32


def dot(left, right):
    return jnp.dot(left, right, preferred_element_type=F32)


def contract_first(left, right):
    return lax.dot_general(left, right, (((0,), (0,)), ((), ())), preferred_element_type=F32)


def contract_last(left, right):
    return lax.dot_general(left, right, (((1,), (1,)), ((), ())), preferred_element_type=F32)


def rope_tables():
    half_size = HEAD_SIZE // 2
    freqs = jnp.exp(-jnp.log(THETA) * (2.0 * jnp.arange(half_size, dtype=F32)) / HEAD_SIZE)
    angles = jnp.arange(SEQUENCE_TOKENS, dtype=F32)[:, None] * freqs[None, :]
    return (jnp.cos(angles), jnp.sin(angles))


def lane_tables():
    cosine, sine = rope_tables()
    return jnp.tile(cosine, (1, 4)), jnp.tile(jnp.concatenate([-sine, sine], axis=1), (1, 2))


def lane_index(shape):
    return lax.broadcasted_iota(jnp.int32, shape, len(shape) - 1)


def swapped(tile):
    half = HEAD_SIZE // 2
    low = lane_index(tile.shape) % HEAD_SIZE < half
    return jnp.where(low, pltpu.roll(tile, LANES - half, 1), pltpu.roll(tile, half, 1))


def spread(tile):
    low = lane_index(tile.shape) < HEAD_SIZE
    moved = pltpu.roll(tile, HEAD_SIZE, 1)
    zero = jnp.zeros_like(tile)
    return [
        jnp.where(low, tile, zero),
        jnp.where(low, zero, moved),
        jnp.where(low, moved, zero),
        jnp.where(low, zero, tile),
    ]


def gathered(spreads):
    return (
        spreads[0]
        + pltpu.roll(spreads[1], HEAD_SIZE, 1)
        + pltpu.roll(spreads[2], HEAD_SIZE, 1)
        + spreads[3]
    )


def causal_mask(shape, key_dim):
    keys = lax.broadcasted_iota(jnp.int32, shape, key_dim)
    queries = lax.broadcasted_iota(jnp.int32, shape, 1 - key_dim)
    return keys <= queries + (shape[key_dim] - shape[1 - key_dim])


def attention_forward_kernel(
    core_ref, near_ref, far_ref, joined_ref, out_ref, first_ref, second_ref,
    kept_ref, given_ref, rows_ref, query_ref, key_ref, value_ref, heads_ref,
    key_spread, value_spread,
):
    core = core_ref[0]
    block = near_ref.shape[0]
    query_width = query_ref.shape[1]
    own = pl.ds(pl.multiple_of(core * block, block), block)
    other = pl.ds(pl.multiple_of((1 - core) * block, block), block)
    rows_ref[own, :] = near_ref[...]
    rows_ref[other, :] = far_ref[...]
    projected = dot(rows_ref[...], joined_ref[...])
    first, second = first_ref[...], second_ref[...]
    for j in range(query_width // LANES):
        tile = projected[:, j * LANES : (j + 1) * LANES]
        query_ref[:, j * LANES : (j + 1) * LANES] = (tile * first + swapped(tile) * second).astype(BF16)
    tile = projected[:, query_width : query_width + LANES]
    key = (tile * first + swapped(tile) * second).astype(BF16)
    value = projected[:, query_width + LANES :].astype(BF16)
    key_ref[...] = key
    value_ref[...] = value
    for i, part in enumerate(spread(key.astype(F32))):
        key_spread[i] = part.astype(BF16)
    for i, part in enumerate(spread(value.astype(F32))):
        value_spread[i] = part.astype(BF16)

    def pair(j, carry):
        lanes = pl.ds(pl.multiple_of(j * LANES, LANES), LANES)
        for begin in range(0, rows_ref.shape[0], TILE):
            end = begin + TILE
            query = query_ref[begin:end, lanes]
            total = jnp.zeros((TILE, LANES), F32)
            for half in range(2):
                index = (2 * j + half) // GROUP * 2 + half
                scores = contract_last(query, key_spread[index, :end, :]) * SCALE
                mask = causal_mask(scores.shape, 1)
                sums = jnp.sum(jnp.where(mask, jnp.exp(scores), 0.0), axis=1, keepdims=True)
                probs = jnp.where(mask, jnp.exp(scores - jnp.log(sums)), 0.0).astype(BF16)
                total = total + dot(probs, value_spread[index, :end, :])
            heads_ref[begin:end, lanes] = total.astype(BF16)
        return carry

    lax.fori_loop(0, query_width // LANES, pair, 0)
    kept_ref[...] = dot(heads_ref[own, :], out_ref[...]).astype(BF16)
    given_ref[...] = dot(heads_ref[other, :], out_ref[...]).astype(BF16)


def vmem():
    return pl.BlockSpec(memory_space=pltpu.VMEM)


def attention_forward(core, near, far, joined, w_out, tables):
    block, width = near.shape
    rows = 2 * block
    query_width = w_out.shape[0]
    shapes = [
        (block, width), (block, width), (rows, width), (rows, query_width),
        (rows, LANES), (rows, LANES), (rows, query_width),
    ]
    flops = 2 * rows * (width * (joined.shape[1] + query_width) + 2 * rows * query_width)
    return pl.pallas_call(
        attention_forward_kernel,
        out_shape=[jax.ShapeDtypeStruct(shape, BF16) for shape in shapes],
        in_specs=[pl.BlockSpec(memory_space=pltpu.SMEM)] + [vmem() for _ in range(6)],
        out_specs=[vmem() for _ in shapes],
        scratch_shapes=[pltpu.VMEM((4, rows, LANES), BF16), pltpu.VMEM((4, rows, LANES), BF16)],
        compiler_params=pltpu.CompilerParams(vmem_limit_bytes=40 << 20),
        cost_estimate=pl.CostEstimate(flops=flops, bytes_accessed=12 << 20, transcendentals=1 << 22),
    )(core, near, far, joined, w_out, *tables)


def attention_backward_kernel(
    core_ref, near_ref, far_ref, joined_ref, out_ref, first_ref, second_ref,
    query_ref, key_ref, value_ref,
    kept_ref, given_ref, rows_ref, projected_ref,
    key_spread, value_spread, key_sum, value_sum, heads,
):
    core = core_ref[0]
    block = near_ref.shape[0]
    query_width = query_ref.shape[1]
    own = pl.ds(pl.multiple_of(core * block, block), block)
    other = pl.ds(pl.multiple_of((1 - core) * block, block), block)
    rows_ref[own, :] = near_ref[...]
    rows_ref[other, :] = far_ref[...]
    heads[...] = contract_last(rows_ref[...], out_ref[...]).astype(BF16)
    for i, part in enumerate(spread(key_ref[...].astype(F32))):
        key_spread[i] = part.astype(BF16)
    for i, part in enumerate(spread(value_ref[...].astype(F32))):
        value_spread[i] = part.astype(BF16)
    key_sum[...] = jnp.zeros_like(key_sum)
    value_sum[...] = jnp.zeros_like(value_sum)

    def pair(j, carry):
        lanes = pl.ds(pl.multiple_of(j * LANES, LANES), LANES)
        for begin in range(0, rows_ref.shape[0], TILE):
            end = begin + TILE
            query = query_ref[begin:end, lanes]
            grad = heads[begin:end, lanes]
            low = lane_index(query.shape) < HEAD_SIZE
            zero = jnp.zeros(query.shape, BF16)
            total = jnp.zeros((TILE, LANES), F32)
            for half in range(2):
                index = (2 * j + half) // GROUP * 2 + half
                key = key_spread[index, :end, :]
                scores = contract_last(key, query) * SCALE
                mask = causal_mask(scores.shape, 0)
                sums = jnp.sum(jnp.where(mask, jnp.exp(scores), 0.0), axis=0, keepdims=True)
                probs = jnp.where(mask, jnp.exp(scores - jnp.log(sums)), 0.0)
                d_probs = contract_last(value_spread[index, :end, :], grad)
                mean = jnp.sum(probs * d_probs, axis=0, keepdims=True)
                d_scores = (probs * (d_probs - mean) * SCALE).astype(BF16)
                mine = low if half == 0 else jnp.logical_not(low)
                value_sum[index, :end, :] += dot(probs.astype(BF16), jnp.where(mine, grad, zero))
                key_sum[index, :end, :] += dot(d_scores, jnp.where(mine, query, zero))
                total = total + contract_first(d_scores, key)
            first, second = first_ref[begin:end, :], second_ref[begin:end, :]
            projected_ref[begin:end, lanes] = (total * first - swapped(total) * second).astype(BF16)
        return carry

    lax.fori_loop(0, query_width // LANES, pair, 0)
    total = gathered([key_sum[i] for i in range(4)])
    projected_ref[:, query_width : query_width + LANES] = (
        total * first_ref[...] - swapped(total) * second_ref[...]
    ).astype(BF16)
    projected_ref[:, query_width + LANES :] = gathered([value_sum[i] for i in range(4)]).astype(BF16)
    kept_ref[...] = contract_last(projected_ref[own, :], joined_ref[...]).astype(BF16)
    given_ref[...] = contract_last(projected_ref[other, :], joined_ref[...]).astype(BF16)


def attention_backward(core, near, far, joined, w_out, tables, query, key, value):
    block, width = near.shape
    rows = 2 * block
    query_width = w_out.shape[0]
    shapes = [(block, width), (block, width), (rows, width), (rows, joined.shape[1])]
    flops = 2 * rows * (width * (joined.shape[1] + query_width) + 5 * rows * query_width)
    return pl.pallas_call(
        attention_backward_kernel,
        out_shape=[jax.ShapeDtypeStruct(shape, BF16) for shape in shapes],
        in_specs=[pl.BlockSpec(memory_space=pltpu.SMEM)] + [vmem() for _ in range(9)],
        out_specs=[vmem() for _ in shapes],
        scratch_shapes=[
            pltpu.VMEM((4, rows, LANES), BF16),
            pltpu.VMEM((4, rows, LANES), BF16),
            pltpu.VMEM((4, rows, LANES), F32),
            pltpu.VMEM((4, rows, LANES), F32),
            pltpu.VMEM((rows, query_width), BF16),
        ],
        compiler_params=pltpu.CompilerParams(vmem_limit_bytes=40 << 20),
        cost_estimate=pl.CostEstimate(flops=flops, bytes_accessed=12 << 20, transcendentals=1 << 22),
    )(core, near, far, joined, w_out, *tables, query, key, value)


def assemble(target, order_ref, base, pieces):
    for i, piece in enumerate(pieces):
        size = piece.shape[1]
        at = pl.multiple_of(order_ref[base + i] * size, size)
        target[pl.ds(at, size), :] = piece[0]


def experts_kernel(
    place_ref, order_ref, tokens_ref, cots_ref, router_ref, gate_ref, *refs, ups, downs
):
    up_refs, down_refs, refs = refs[:ups], refs[ups : ups + downs], refs[ups + downs :]
    (moe_ref, back_ref, gates_ref, gated_ref, d_gate_ref, d_up_ref,
     up, down, moe_sum, back_sum, d_gates) = refs
    expert, tile = pl.program_id(0), pl.program_id(1)
    width = tokens_ref.shape[1]
    rows = pl.ds(pl.multiple_of(tile * TILE, TILE), TILE)
    lane = place_ref[0] + expert

    @pl.when(tile == 0)
    def _():
        assemble(up, order_ref, 0, up_refs)
        assemble(down, order_ref, ups, down_refs)

    tokens = tokens_ref[rows, :]
    cots = cots_ref[rows, :width]

    @pl.when(expert == 0)
    def _():
        logits = dot(tokens, router_ref[...])
        raised = jnp.where(cots_ref[rows, width:] > 0.5, jnp.exp(logits), 0.0)
        gates_ref[rows, :] = raised / jnp.sum(raised, axis=1, keepdims=True)
        d_gates[rows, :] = jnp.zeros((TILE, LANES), F32)
        moe_sum[rows, :] = jnp.zeros((TILE, width), F32)
        back_sum[rows, :] = jnp.zeros((TILE, width), F32)

    chosen = lane_index((TILE, LANES)) == lane
    gates = jnp.sum(jnp.where(chosen, gates_ref[rows, :], 0.0), axis=1, keepdims=True)
    gate_act = dot(tokens, gate_ref[0])
    up_act = dot(tokens, up[...])
    sigmoid = jax.nn.sigmoid(gate_act)
    silu = gate_act * sigmoid
    middle = silu * up_act
    gated = (gates * middle).astype(BF16)
    gated_ref[0] = gated
    moe_sum[rows, :] += dot(gated, down[...])
    plain = contract_last(cots, down[...])
    d_gate = jnp.sum(plain * middle, axis=1, keepdims=True)
    d_gates[rows, :] += jnp.where(chosen, d_gate, 0.0)
    d_middle = plain * gates
    d_gate_act = (d_middle * up_act * sigmoid * (1.0 + gate_act * (1.0 - sigmoid))).astype(BF16)
    d_up_act = (d_middle * silu).astype(BF16)
    d_gate_ref[0] = d_gate_act
    d_up_ref[0] = d_up_act
    back_sum[rows, :] += contract_last(d_gate_act, gate_ref[0]) + contract_last(d_up_act, up[...])

    @pl.when(expert == pl.num_programs(0) - 1)
    def _():
        moe_ref[rows, :] = moe_sum[rows, :].astype(BF16)
        back_ref[rows, :width] = back_sum[rows, :].astype(BF16)
        whole = d_gates[rows, :]
        high = whole.astype(BF16).astype(F32)
        back_ref[rows, width:] = (high + pltpu.roll(whole - high, LANES // 2, 1)).astype(BF16)


def experts(place, order, tokens, cots, router, w_gate, up_pieces, down_pieces):
    count, width = tokens.shape
    owned, _, hidden = w_gate.shape

    def whole(shape):
        return pl.BlockSpec(shape, lambda e, t, *_: (0, 0))

    def expert(array):
        return pl.BlockSpec((1,) + array.shape[1:], lambda e, t, *_: (e, 0, 0))

    rows_spec = pl.BlockSpec((1, TILE, hidden), lambda e, t, *_: (e, t, 0))
    products = jax.ShapeDtypeStruct((owned, count, hidden), BF16)
    pieces = (*up_pieces, *down_pieces)
    return pl.pallas_call(
        functools.partial(experts_kernel, ups=len(up_pieces), downs=len(down_pieces)),
        out_shape=[
            jax.ShapeDtypeStruct((count, width), BF16),
            jax.ShapeDtypeStruct((count, width + LANES), BF16),
            jax.ShapeDtypeStruct((count, LANES), F32),
            products, products, products,
        ],
        grid_spec=pltpu.PrefetchScalarGridSpec(
            num_scalar_prefetch=2,
            grid=(owned, count // TILE),
            in_specs=[
                whole(tokens.shape), whole(cots.shape), whole(router.shape), expert(w_gate),
                *(expert(piece) for piece in pieces),
            ],
            out_specs=[
                whole((count, width)), whole((count, width + LANES)), whole((count, LANES)),
                rows_spec, rows_spec, rows_spec,
            ],
            scratch_shapes=[
                pltpu.VMEM((width, hidden), BF16),
                pltpu.VMEM((hidden, width), BF16),
                pltpu.VMEM((count, width), F32),
                pltpu.VMEM((count, width), F32),
                pltpu.VMEM((count, LANES), F32),
            ],
        ),
        compiler_params=pltpu.CompilerParams(vmem_limit_bytes=58 << 20),
        cost_estimate=pl.CostEstimate(
            flops=12 * count * width * hidden * owned,
            bytes_accessed=6 * width * hidden * owned + 24 * count * width,
            transcendentals=count * hidden * owned,
        ),
    )(place, order, tokens, cots, router, w_gate, *pieces)


def shares_kernel(order_ref, *refs, groups, entries, added):
    for i in range(entries):
        total = None
        for group in range(groups):
            start = group * (entries + 1)
            left, right = refs[start + i], refs[start + entries]
            left = left[...] if len(left.shape) == 2 else left[0]
            right = right[...] if len(right.shape) == 2 else right[0]
            part = contract_first(left, right)
            total = part if total is None else total + part
        if added:
            total = total + refs[groups * (entries + 1)][i, 0].astype(F32)
        refs[-1][i, 0] = total.astype(BF16)


def shares(order, groups, rows, added=None):
    entries = order.shape[0]
    specs, operands = [], []
    for left, right in groups:
        for i in range(entries):
            if left.ndim == 2:
                specs.append(pl.BlockSpec((left.shape[0], rows), lambda e, o, i=i: (0, o[i])))
            else:
                specs.append(
                    pl.BlockSpec((1, left.shape[1], rows), lambda e, o, i=i: (e, 0, o[i]))
                )
            operands.append(left)
        if right.ndim == 2:
            specs.append(pl.BlockSpec(right.shape, lambda e, o: (0, 0)))
        else:
            specs.append(pl.BlockSpec((1,) + right.shape[1:], lambda e, o: (e, 0, 0)))
        operands.append(right)
    owned = max(array.shape[0] for array in groups[0] if array.ndim == 3)
    columns = groups[0][1].shape[-1]
    block = pl.BlockSpec((entries, 1, rows, columns), lambda e, o: (0, e, 0, 0))
    if added is not None:
        specs.append(block)
        operands.append(added)
    tokens = sum(left.shape[-2] for left, _ in groups)
    return pl.pallas_call(
        functools.partial(
            shares_kernel, groups=len(groups), entries=entries, added=added is not None
        ),
        out_shape=jax.ShapeDtypeStruct((entries, owned, rows, columns), BF16),
        grid_spec=pltpu.PrefetchScalarGridSpec(
            num_scalar_prefetch=1, grid=(owned,), in_specs=specs, out_specs=block
        ),
        compiler_params=pltpu.CompilerParams(vmem_limit_bytes=40 << 20),
        cost_estimate=pl.CostEstimate(
            flops=2 * tokens * rows * columns * owned * entries,
            bytes_accessed=4 * owned * entries * rows * columns + 6 * tokens * columns * owned,
            transcendentals=0,
        ),
    )(order, *operands)


def rotate(tensor, cosine_table, sine_table):
    half_size = tensor.shape[-1] // 2
    first = tensor[..., :half_size]
    second = tensor[..., half_size:]
    return jnp.concatenate(
        [first * cosine_table - second * sine_table, second * cosine_table + first * sine_table],
        axis=-1,
    )


def plain_scores(query_rows, key_rows):
    scores = (
        jnp.einsum("skgqd,skvd->skgqv", query_rows, key_rows, preferred_element_type=F32) * SCALE
    )
    positions = jnp.arange(SEQUENCE_TOKENS, dtype=jnp.int32)
    causal = positions[:, None] >= positions[None, :]
    total = jnp.sum(jnp.where(causal, jnp.exp(scores), 0.0), axis=-1, keepdims=True)
    return jnp.where(causal, jnp.exp(scores - jnp.log(total)), 0.0)


def plain_forward(normed_all, joined, w_out):
    query_width = w_out.shape[0]
    kv_local = query_width // GROUP // HEAD_SIZE
    cosine_table, sine_table = rope_tables()
    projected = dot(normed_all, joined)
    split = (-1, SEQUENCE_TOKENS, kv_local)
    query = projected[:, :query_width].reshape(*split, GROUP, HEAD_SIZE).transpose(0, 2, 3, 1, 4)
    key, value = (
        part.reshape(*split, HEAD_SIZE).transpose(0, 2, 1, 3)
        for part in jnp.split(projected[:, query_width:], 2, axis=1)
    )
    value = value.astype(BF16)
    query = rotate(query, cosine_table, sine_table).astype(BF16)
    key = rotate(key, cosine_table, sine_table).astype(BF16)
    probs = plain_scores(query, key).astype(BF16)
    heads = jnp.einsum("skgqv,skvd->skgqd", probs, value, preferred_element_type=F32)
    heads = heads.astype(BF16).transpose(0, 3, 1, 2, 4).reshape(-1, query_width)
    return dot(heads, w_out), query, key, value, heads


def plain_backward(d_attn_all, w_out, query, key, value):
    query_width = w_out.shape[0]
    rows = d_attn_all.shape[0]
    kv_local = query_width // GROUP // HEAD_SIZE
    cosine_table, sine_table = rope_tables()
    grad = contract_last(d_attn_all, w_out).astype(BF16)
    grad = grad.reshape(-1, SEQUENCE_TOKENS, kv_local, GROUP, HEAD_SIZE).transpose(0, 2, 3, 1, 4)
    probs = plain_scores(query, key)
    d_value = jnp.einsum(
        "skgqv,skgqd->skvd", probs.astype(BF16), grad, preferred_element_type=F32
    )
    d_probs = jnp.einsum("skgqd,skvd->skgqv", grad, value, preferred_element_type=F32)
    d_scores = (
        probs * (d_probs - jnp.sum(probs * d_probs, axis=-1, keepdims=True)) * SCALE
    ).astype(BF16)
    d_query = jnp.einsum("skgqv,skvd->skgqd", d_scores, key, preferred_element_type=F32)
    d_key = jnp.einsum("skgqv,skgqd->skvd", d_scores, query, preferred_element_type=F32)
    d_query = rotate(d_query, cosine_table, -sine_table).astype(BF16).transpose(0, 3, 1, 2, 4)
    d_key = rotate(d_key, cosine_table, -sine_table).astype(BF16).transpose(0, 2, 1, 3)
    d_value = d_value.astype(BF16).transpose(0, 2, 1, 3)
    return jnp.concatenate([part.reshape(rows, -1) for part in (d_query, d_key, d_value)], axis=1)


def normalize(row_data):
    inverse = lax.rsqrt(jnp.mean(row_data * row_data, axis=-1, keepdims=True) + EPS)
    return (row_data * inverse, inverse)


def normalize_back(d_normed, normal_hat, inverse, gain):
    d_hat = d_normed * gain
    return inverse * (d_hat - normal_hat * jnp.mean(d_hat * normal_hat, axis=-1, keepdims=True))


def after(value, *earlier):
    return lax.optimization_barrier((value, *earlier))[0] if earlier else value


def add(*parts):
    return sum(part.astype(F32) for part in parts)


class Axis:
    def __init__(self, name, size):
        self.name = name
        self.size = size
        self.mine = lax.axis_index(name)

    def fetch(self, value, distance):
        n = self.size
        return lax.ppermute(value, self.name, [((i + distance) % n, i) for i in range(n)])

    def deliver(self, value, distance):
        n = self.size
        return lax.ppermute(value, self.name, [(i, (i + distance) % n) for i in range(n)])


class Tensor:
    def __init__(self, size):
        self.size = size
        self.halves = size // 2
        self.mine = lax.axis_index("tensor")
        self.half = self.mine // 2
        self.core = self.mine % 2

    def swap_core(self, value):
        return lax.ppermute(value, "tensor", [(t, t ^ 1) for t in range(self.size)])

    def shift_half(self, value, step):
        n = self.halves
        return lax.ppermute(
            value, "tensor", [(t, (t // 2 + step) % n * 2 + t % 2) for t in range(self.size)]
        )

    def order(self):
        places = []
        for step in range(self.halves):
            half = (self.half - step) % self.halves
            places += [half * 2 + self.core, half * 2 + 1 - self.core]
        return places

    def gather(self, value):
        mine = [value] + [self.shift_half(value, step) for step in range(1, self.halves)]
        pieces = [piece for one in mine for piece in (one, self.swap_core(one))]
        out = jnp.zeros((self.size,) + value.shape, value.dtype)
        for place, piece in zip(self.order(), pieces):
            out = lax.dynamic_update_slice(out, piece[None], (place,) + (0,) * value.ndim)
        return out

    def scatter(self, stacked):
        n = self.halves
        view = stacked.reshape((n, 2) + stacked.shape[1:])
        kept = lax.dynamic_index_in_dim(view, self.core, 1, keepdims=False)
        given = lax.dynamic_index_in_dim(view, 1 - self.core, 1, keepdims=False)
        pair = add(kept, self.swap_core(given))
        total = lax.dynamic_index_in_dim(pair, self.half, 0, keepdims=False)
        for step in range(1, n):
            part = lax.dynamic_index_in_dim(pair, (self.half + step) % n, 0, keepdims=False)
            total = add(total, self.shift_half(part.astype(BF16), step))
        return total


def swap_all(value, sizes):
    for axis, size in sizes:
        bit = 1
        while bit < size:
            value = value + lax.ppermute(value, axis, [(i, i ^ bit) for i in range(size)])
            bit *= 2
    return value


def fetch_weight(ring, copies, weight, *hold):
    size = weight.shape[1] // copies.size
    part = lax.dynamic_slice_in_dim(weight, copies.mine * size, size, 1)
    part = after(part, *hold)
    pieces = [(weight, ring.half, 1, 0)]
    for step in range(1, ring.halves):
        got = ring.shift_half(part, step)
        half = (ring.half - step) % ring.halves
        pieces.append((got, half, copies.size, copies.mine))
        for k in range(1, copies.size):
            other = (copies.mine + k) % copies.size
            pieces.append((copies.fetch(got, k), half, copies.size, other))
    arrays, places = [], []
    for core, swap in ((ring.core, False), (1 - ring.core, True)):
        for array, half, parts, part in pieces:
            arrays.append(ring.swap_core(array) if swap else array)
            places.append((half * 2 + core) * parts + part)
    return arrays, places


def shared_grads(ring, groups, rows):
    order = ring.order()

    def part(places, added):
        if rows % LANES == 0:
            return shares(jnp.stack(places).astype(jnp.int32), groups, rows, added)
        blocks = []
        for place in places:
            total = None
            for left, right in groups:
                left = lax.dynamic_slice_in_dim(left, place * rows, rows, left.ndim - 1)
                sums = "td,etf->edf" if left.ndim == 2 else "etd,tf->edf"
                one = jnp.einsum(sums, left, right, preferred_element_type=F32)
                total = one if total is None else total + one
            blocks.append(total)
        stacked = jnp.stack(blocks)
        return (stacked if added is None else add(stacked, added)).astype(BF16)

    given = part(order[1::2], None)
    return part(order[0::2], ring.swap_core(given))


def local(
    sizes,
    layer_input,
    norm1_gain,
    w_query,
    key_matrix,
    value_matrix,
    w_out,
    norm2_gain,
    w_router,
    w_gate,
    w_up,
    w_down,
    routes,
    cotangent,
):
    row_count, width = layer_input.shape
    expert_total = w_router.shape[1]
    owned = w_gate.shape[0]
    ring = Tensor(sizes["tensor"])
    line = Axis("expert", sizes["expert"])
    copies = Axis("dp", sizes["dp"])
    query_width = w_query.shape[1]
    kv_width = key_matrix.shape[1]
    by_kernel = (
        2 * row_count == SEQUENCE_TOKENS and query_width % LANES == 0 and kv_width == LANES
    )
    core = ring.core.astype(jnp.int32)[None]

    row_float = layer_input.astype(F32)
    hat_one, inverse_one = normalize(row_float)
    normed_one = (hat_one * norm1_gain).astype(BF16)
    joined = jnp.concatenate([w_query, key_matrix, value_matrix], axis=1)
    tables = lane_tables()
    named = jnp.sum(
        (routes[:, :, None] == jnp.arange(LANES, dtype=jnp.int32)).astype(BF16), axis=1
    )
    cots = jnp.concatenate([cotangent, named], axis=1)
    cots_of = {k: line.fetch(cots, k) if k else cots for k in range(line.size)}
    if by_kernel:
        partner = ring.swap_core(normed_one)
        across = ring.shift_half(normed_one, 1)
        across_partner = ring.swap_core(across)
        down_pieces, down_places = fetch_weight(ring, copies, w_down, across)
        near = attention_forward(core, normed_one, partner, joined, w_out, tables)
        far = attention_forward(core, across, across_partner, joined, w_out, tables)
        far_sum = add(far[0], ring.swap_core(far[1])).astype(BF16)
        last = ring.shift_half(far_sum, 1)
        attended = add(near[0], ring.swap_core(near[1]), last)
    else:
        normed_all = ring.gather(normed_one).reshape(-1, width)
        down_pieces, down_places = fetch_weight(ring, copies, w_down, normed_all)
        attended, query, key, value, heads = plain_forward(normed_all, joined, w_out)
        attended = ring.scatter(attended.reshape(ring.size, row_count, width))
        last = attended
    hidden = row_float + attended

    hat_two, inverse_two = normalize(hidden)
    normed_two = (hat_two * norm2_gain).astype(BF16)
    gate_all = lax.all_gather(after(w_gate, last), "tensor", axis=1, tiled=True)
    up_pieces, up_places = fetch_weight(ring, copies, w_up, last)
    order = jnp.stack(up_places + down_places).astype(jnp.int32)
    middle = line.size // 2
    early = list(range(0, line.size, middle))
    late = [k for k in range(line.size) if k % middle]
    tokens_of = {k: line.fetch(normed_two, k) if k else normed_two for k in early}
    held = after(normed_two, *(tokens_of[k] for k in early[1:]))
    tokens_of.update({k: line.fetch(held, k) for k in late})
    router = jnp.pad(w_router, ((0, 0), (0, LANES - expert_total)))
    place = (line.mine * owned).astype(jnp.int32)[None]

    moe_of, back_of, token_groups, cot_groups, products = {}, {}, [], [], []
    for group in (early, late):
        rows = jnp.concatenate([tokens_of[k] for k in group], axis=0)
        grads = jnp.concatenate([cots_of[k] for k in group], axis=0)
        moe, back, gates_group, *made = experts(
            place, order, rows, grads, router, gate_all, up_pieces, down_pieces
        )
        if 0 in group:
            gates = gates_group[:row_count]
        for i, k in enumerate(group):
            moe_of[k] = moe[i * row_count : (i + 1) * row_count]
            back_of[k] = back[i * row_count : (i + 1) * row_count]
        token_groups.append(rows)
        cot_groups.append(grads)
        products.append(made)
    backs = [back_of[0]] + [line.deliver(back_of[k], k) for k in range(1, line.size)]
    back = add(*backs)
    d_normed_two = back[:, :width]
    d_gates = back[:, width : width + LANES // 2] + back[:, width + LANES // 2 :]
    moes = [moe_of[0]] + [line.deliver(after(moe_of[k], *backs), k) for k in range(1, line.size)]
    layer_output = (hidden + add(*moes)).astype(BF16)

    gated, d_gate_act, d_up_act = ([made[i] for made in products] for i in range(3))
    gate_kept = shared_grads(ring, list(zip(token_groups, d_gate_act)), w_gate.shape[1])
    up_kept = shared_grads(ring, list(zip(token_groups, d_up_act)), w_up.shape[1])
    down_kept = shared_grads(
        ring, [(a, b[:, :width]) for a, b in zip(gated, cot_groups)], w_down.shape[1]
    )

    gates = gates[:, : LANES // 2]
    d_logits = (gates * (d_gates - jnp.sum(gates * d_gates, axis=-1, keepdims=True))).astype(BF16)
    grad_router = contract_first(d_logits, normed_two)[:expert_total]
    d_normed_two = d_normed_two + contract_last(d_logits, router[:, : LANES // 2])
    grad_norm2 = jnp.sum(d_normed_two * hat_two, axis=0)
    d_hidden = cotangent.astype(F32) + normalize_back(
        d_normed_two, hat_two, inverse_two, norm2_gain
    )

    d_attn = d_hidden.astype(BF16)
    if by_kernel:
        d_partner = ring.swap_core(d_attn)
        d_across = ring.shift_half(d_attn, 1)
        d_across_partner = ring.swap_core(d_across)
        near_back = attention_backward(core, d_attn, d_partner, joined, w_out, tables, *near[3:6])
        far_back = attention_backward(
            core, d_across, d_across_partner, joined, w_out, tables, *far[3:6]
        )
        far_sum = add(far_back[0], ring.swap_core(far_back[1])).astype(BF16)
        d_normed_one = add(near_back[0], ring.swap_core(near_back[1]), ring.shift_half(far_sum, 1))
        grad_out = contract_first(near[6], near_back[2]) + contract_first(far[6], far_back[2])
        grad_joined = contract_first(near[2], near_back[3]) + contract_first(far[2], far_back[3])
        turn = near_back[0]
    else:
        d_attn_all = ring.gather(d_attn).reshape(-1, width)
        d_projected = plain_backward(d_attn_all, w_out, query, key, value)
        d_normed_one = ring.scatter(
            contract_last(d_projected, joined).reshape(ring.size, row_count, width)
        )
        grad_out = contract_first(heads, d_attn_all)
        grad_joined = contract_first(normed_all, d_projected)
        turn = d_projected
    grad_norm1 = jnp.sum(d_normed_one * hat_one, axis=0)
    d_input = d_hidden + normalize_back(d_normed_one, hat_one, inverse_one, norm1_gain)

    grad_joined, grad_out = (
        grad.astype(F32)
        for grad in lax.psum((grad_joined.astype(BF16), grad_out.astype(BF16)), ("dp", "expert"))
    )
    grad_query = grad_joined[:, :query_width]
    grad_key = grad_joined[:, query_width : query_width + kv_width]
    grad_value = grad_joined[:, query_width + kv_width :]

    pad = -(expert_total + 2) % 16
    small = jnp.concatenate([grad_router, grad_norm2[None], grad_norm1[None]], axis=0)
    small = jnp.pad(small, ((0, pad), (0, 0)))
    small = small + ring.swap_core(small)
    small = swap_all(small, [("expert", line.size)])
    if ring.halves > 2:
        bits = [1 << i for i in range(1, ring.halves.bit_length())]
        for bit in bits:
            small = small + lax.ppermute(small, "tensor", [(t, t ^ bit) for t in range(ring.size)])

    def over_halves(kept, hold, rider=None):
        total, received = kept[0], []
        for step in range(1, ring.halves):
            part = after(kept[step], *hold)
            shape = part.shape
            if rider is not None:
                part = jnp.concatenate([part.reshape(-1, width), rider], axis=0)
            got = ring.shift_half(part, ring.halves - step)
            if rider is not None:
                received.append(got[-rider.shape[0] :])
                got = got[: -rider.shape[0]].reshape(shape)
            total = add(total, got)
            hold = (got,)
        return total.astype(BF16), hold, received

    gate_total, hold, _ = over_halves(gate_kept, (turn,)[:0])
    up_total, hold, _ = over_halves(up_kept, hold + (turn,))
    low = small.astype(BF16)
    if ring.halves == 2:
        down_total, _, received = over_halves(down_kept, hold, low)
        low = add(low, received[0]).astype(BF16)
    else:
        down_total, _, _ = over_halves(down_kept, hold)

    def exchanged(total):
        for k in range(1, copies.size):
            total = add(total, copies.fetch(total, k))
        return total

    grad_gate = exchanged(gate_total)
    grad_up = exchanged(up_total)
    shape = down_total.shape
    mixed = exchanged(jnp.concatenate([down_total.reshape(-1, width), low], axis=0))
    grad_down = mixed[: -low.shape[0]].reshape(shape)
    small = mixed[-low.shape[0] :]
    return (
        layer_output,
        d_input,
        small[expert_total + 1],
        grad_query,
        grad_key,
        grad_value,
        grad_out,
        small[expert_total],
        small[:expert_total].T,
        grad_gate,
        grad_up,
        grad_down,
    )


def solution(mesh):
    in_specs = (
        P(("dp", "expert", "tensor"), None),
        P(),
        P(None, "tensor"),
        P(None, "tensor"),
        P(None, "tensor"),
        P("tensor", None),
        P(),
        P(),
        P("expert", "tensor", None),
        P("expert", "tensor", None),
        P("expert", "tensor", None),
        P(("dp", "expert", "tensor"), None),
        P(("dp", "expert", "tensor"), None),
    )
    out_specs = (
        P(("dp", "expert", "tensor"), None),
        P(("dp", "expert", "tensor"), None),
        P(),
        P(None, "tensor"),
        P(None, "tensor"),
        P(None, "tensor"),
        P("tensor", None),
        P(),
        P(),
        P("expert", "tensor", None),
        P("expert", "tensor", None),
        P("expert", "tensor", None),
    )

    def step(*args):
        return local(dict(mesh.shape), *args)

    return jax.shard_map(
        step, mesh=mesh, in_specs=in_specs, out_specs=out_specs, check_vma=False
    )
```

```python
import functools
import math

import jax
import jax.numpy as jnp
from jax import lax
from jax.experimental import pallas as pl
from jax.experimental.pallas import tpu as pltpu
from jax.sharding import PartitionSpec as P


QUERY_HEADS = 24
KEY_VALUE_HEADS = 8
HEAD_SIZE = 64
SEQUENCE_TOKENS = 512
LANES = 128
TILE = 256

EPS = 1e-06
THETA = 10000.0
SCALE = 1.0 / math.sqrt(HEAD_SIZE)
GROUP = QUERY_HEADS // KEY_VALUE_HEADS
BF16 = jnp.bfloat16
F32 = jnp.float32


def dot(left, right):
    return jnp.dot(left, right, preferred_element_type=F32)


def contract_first(left, right):
    return lax.dot_general(left, right, (((0,), (0,)), ((), ())), preferred_element_type=F32)


def contract_last(left, right):
    return lax.dot_general(left, right, (((1,), (1,)), ((), ())), preferred_element_type=F32)


def rope_tables(lanes=HEAD_SIZE // 2):
    pairs = (jnp.arange(lanes, dtype=jnp.int32) % (HEAD_SIZE // 2)).astype(F32)
    freqs = jnp.exp(-jnp.log(THETA) * (2.0 * pairs) / HEAD_SIZE)
    angles = jnp.arange(SEQUENCE_TOKENS, dtype=F32)[:, None] * freqs[None, :]
    return (jnp.cos(angles), jnp.sin(angles))


def lane_tables():
    cosine, sine = rope_tables(LANES)
    return cosine, jnp.where(lane_index(sine.shape) % HEAD_SIZE < HEAD_SIZE // 2, -sine, sine)


def lane_index(shape):
    return lax.broadcasted_iota(jnp.int32, shape, len(shape) - 1)


def swapped(tile):
    half = HEAD_SIZE // 2
    low = lane_index(tile.shape) % HEAD_SIZE < half
    return jnp.where(low, pltpu.roll(tile, LANES - half, 1), pltpu.roll(tile, half, 1))


def spread(tile):
    low = lane_index(tile.shape) < HEAD_SIZE
    moved = pltpu.roll(tile, HEAD_SIZE, 1)
    zero = jnp.zeros_like(tile)
    return [
        jnp.where(low, tile, zero),
        jnp.where(low, zero, moved),
        jnp.where(low, moved, zero),
        jnp.where(low, zero, tile),
    ]


def gathered(spreads):
    return (
        spreads[0]
        + pltpu.roll(spreads[1], HEAD_SIZE, 1)
        + pltpu.roll(spreads[2], HEAD_SIZE, 1)
        + spreads[3]
    )


def causal_mask(shape, key_dim):
    keys = lax.broadcasted_iota(jnp.int32, shape, key_dim)
    queries = lax.broadcasted_iota(jnp.int32, shape, 1 - key_dim)
    return keys <= queries + (shape[key_dim] - shape[1 - key_dim])


def join(target, parts):
    at = 0
    for part in parts:
        target[:, at : at + part.shape[1]] = part[...]
        at += part.shape[1]


def attention_forward_kernel(
    core_ref, near_ref, far_ref, *refs
):
    weights, refs = refs[:3], refs[3:]
    (out_ref, first_ref, second_ref,
     kept_ref, given_ref, rows_ref, query_ref, key_ref, value_ref, heads_ref,
     key_spread, value_spread, joined_ref) = refs
    join(joined_ref, weights)
    core = core_ref[0]
    block = near_ref.shape[0]
    query_width = query_ref.shape[1]
    own = pl.ds(pl.multiple_of(core * block, block), block)
    other = pl.ds(pl.multiple_of((1 - core) * block, block), block)
    rows_ref[own, :] = near_ref[...]
    rows_ref[other, :] = far_ref[...]
    projected = dot(rows_ref[...], joined_ref[...])
    first, second = first_ref[...], second_ref[...]
    for j in range(query_width // LANES):
        tile = projected[:, j * LANES : (j + 1) * LANES]
        query_ref[:, j * LANES : (j + 1) * LANES] = (tile * first + swapped(tile) * second).astype(BF16)
    tile = projected[:, query_width : query_width + LANES]
    key = (tile * first + swapped(tile) * second).astype(BF16)
    value = projected[:, query_width + LANES :].astype(BF16)
    key_ref[...] = key
    value_ref[...] = value
    for i, part in enumerate(spread(key.astype(F32))):
        key_spread[i] = part.astype(BF16)
    for i, part in enumerate(spread(value.astype(F32))):
        value_spread[i] = part.astype(BF16)

    def pair(j, carry):
        lanes = pl.ds(pl.multiple_of(j * LANES, LANES), LANES)
        for begin in range(0, rows_ref.shape[0], TILE):
            end = begin + TILE
            query = query_ref[begin:end, lanes]
            total = jnp.zeros((TILE, LANES), F32)
            for half in range(2):
                index = (2 * j + half) // GROUP * 2 + half
                scores = contract_last(query, key_spread[index, :end, :]) * SCALE
                mask = causal_mask(scores.shape, 1)
                sums = jnp.sum(jnp.where(mask, jnp.exp(scores), 0.0), axis=1, keepdims=True)
                probs = jnp.where(mask, jnp.exp(scores - jnp.log(sums)), 0.0).astype(BF16)
                total = total + dot(probs, value_spread[index, :end, :])
            heads_ref[begin:end, lanes] = total.astype(BF16)
        return carry

    lax.fori_loop(0, query_width // LANES, pair, 0)
    kept_ref[...] = dot(heads_ref[own, :], out_ref[...]).astype(BF16)
    given_ref[...] = dot(heads_ref[other, :], out_ref[...]).astype(BF16)


def vmem():
    return pl.BlockSpec(memory_space=pltpu.VMEM)


def attention_forward(core, near, far, weights, w_out, tables):
    block, width = near.shape
    rows = 2 * block
    query_width = w_out.shape[0]
    joined = (width, sum(part.shape[1] for part in weights))
    shapes = [
        (block, width), (block, width), (rows, width), (rows, query_width),
        (rows, LANES), (rows, LANES), (rows, query_width),
    ]
    flops = 2 * rows * (width * (joined[1] + query_width) + 2 * rows * query_width)
    return pl.pallas_call(
        attention_forward_kernel,
        out_shape=[jax.ShapeDtypeStruct(shape, BF16) for shape in shapes],
        in_specs=[pl.BlockSpec(memory_space=pltpu.SMEM)] + [vmem() for _ in range(8)],
        out_specs=[vmem() for _ in shapes],
        scratch_shapes=[
            pltpu.VMEM((4, rows, LANES), BF16),
            pltpu.VMEM((4, rows, LANES), BF16),
            pltpu.VMEM(joined, BF16),
        ],
        compiler_params=pltpu.CompilerParams(vmem_limit_bytes=40 << 20),
        cost_estimate=pl.CostEstimate(flops=flops, bytes_accessed=12 << 20, transcendentals=1 << 22),
    )(core, near, far, *weights, w_out, *tables)


def attention_backward_kernel(
    core_ref, near_ref, far_ref, *refs
):
    weights, refs = refs[:3], refs[3:]
    (out_ref, first_ref, second_ref, query_ref, key_ref, value_ref,
     kept_ref, given_ref, rows_ref, projected_ref,
     key_spread, value_spread, key_sum, value_sum, heads, joined_ref) = refs
    join(joined_ref, weights)
    core = core_ref[0]
    block = near_ref.shape[0]
    query_width = query_ref.shape[1]
    own = pl.ds(pl.multiple_of(core * block, block), block)
    other = pl.ds(pl.multiple_of((1 - core) * block, block), block)
    rows_ref[own, :] = near_ref[...]
    rows_ref[other, :] = far_ref[...]
    heads[...] = contract_last(rows_ref[...], out_ref[...]).astype(BF16)
    for i, part in enumerate(spread(key_ref[...].astype(F32))):
        key_spread[i] = part.astype(BF16)
    for i, part in enumerate(spread(value_ref[...].astype(F32))):
        value_spread[i] = part.astype(BF16)
    key_sum[...] = jnp.zeros_like(key_sum)
    value_sum[...] = jnp.zeros_like(value_sum)

    def pair(j, carry):
        lanes = pl.ds(pl.multiple_of(j * LANES, LANES), LANES)
        for begin in range(0, rows_ref.shape[0], TILE):
            end = begin + TILE
            query = query_ref[begin:end, lanes]
            grad = heads[begin:end, lanes]
            low = lane_index(query.shape) < HEAD_SIZE
            zero = jnp.zeros(query.shape, BF16)
            total = jnp.zeros((TILE, LANES), F32)
            for half in range(2):
                index = (2 * j + half) // GROUP * 2 + half
                key = key_spread[index, :end, :]
                scores = contract_last(key, query) * SCALE
                mask = causal_mask(scores.shape, 0)
                sums = jnp.sum(jnp.where(mask, jnp.exp(scores), 0.0), axis=0, keepdims=True)
                probs = jnp.where(mask, jnp.exp(scores - jnp.log(sums)), 0.0)
                d_probs = contract_last(value_spread[index, :end, :], grad)
                mean = jnp.sum(probs * d_probs, axis=0, keepdims=True)
                d_scores = (probs * (d_probs - mean) * SCALE).astype(BF16)
                mine = low if half == 0 else jnp.logical_not(low)
                value_sum[index, :end, :] += dot(probs.astype(BF16), jnp.where(mine, grad, zero))
                key_sum[index, :end, :] += dot(d_scores, jnp.where(mine, query, zero))
                total = total + contract_first(d_scores, key)
            first, second = first_ref[begin:end, :], second_ref[begin:end, :]
            projected_ref[begin:end, lanes] = (total * first - swapped(total) * second).astype(BF16)
        return carry

    lax.fori_loop(0, query_width // LANES, pair, 0)
    total = gathered([key_sum[i] for i in range(4)])
    projected_ref[:, query_width : query_width + LANES] = (
        total * first_ref[...] - swapped(total) * second_ref[...]
    ).astype(BF16)
    projected_ref[:, query_width + LANES :] = gathered([value_sum[i] for i in range(4)]).astype(BF16)
    kept_ref[...] = contract_last(projected_ref[own, :], joined_ref[...]).astype(BF16)
    given_ref[...] = contract_last(projected_ref[other, :], joined_ref[...]).astype(BF16)


def attention_backward(core, near, far, weights, w_out, tables, query, key, value):
    block, width = near.shape
    rows = 2 * block
    query_width = w_out.shape[0]
    joined = (width, sum(part.shape[1] for part in weights))
    shapes = [(block, width), (block, width), (rows, width), (rows, joined[1])]
    flops = 2 * rows * (width * (joined[1] + query_width) + 5 * rows * query_width)
    return pl.pallas_call(
        attention_backward_kernel,
        out_shape=[jax.ShapeDtypeStruct(shape, BF16) for shape in shapes],
        in_specs=[pl.BlockSpec(memory_space=pltpu.SMEM)] + [vmem() for _ in range(11)],
        out_specs=[vmem() for _ in shapes],
        scratch_shapes=[
            pltpu.VMEM((4, rows, LANES), BF16),
            pltpu.VMEM((4, rows, LANES), BF16),
            pltpu.VMEM((4, rows, LANES), F32),
            pltpu.VMEM((4, rows, LANES), F32),
            pltpu.VMEM((rows, query_width), BF16),
            pltpu.VMEM(joined, BF16),
        ],
        compiler_params=pltpu.CompilerParams(vmem_limit_bytes=40 << 20),
        cost_estimate=pl.CostEstimate(flops=flops, bytes_accessed=12 << 20, transcendentals=1 << 22),
    )(core, near, far, *weights, w_out, *tables, query, key, value)


def assemble(target, order_ref, base, pieces):
    for i, piece in enumerate(pieces):
        size = piece.shape[1]
        at = pl.multiple_of(order_ref[base + i] * size, size)
        target[pl.ds(at, size), :] = piece[0]


def experts_kernel(place_ref, order_ref, *refs, blocks, counts):
    token_refs, cot_refs, refs = refs[:blocks], refs[blocks : 2 * blocks], refs[2 * blocks :]
    router_ref, pieces, refs = refs[0], refs[1 : 1 + sum(counts)], refs[1 + sum(counts) :]
    moe_refs, back_refs, refs = refs[:blocks], refs[blocks : 2 * blocks], refs[2 * blocks :]
    (tokens_ref, cots_ref, gates_ref, gated_ref, d_gate_ref, d_up_ref,
     named, gate, up, down, moe_sum, back_sum, d_gates) = refs
    expert, tile = pl.program_id(0), pl.program_id(1)
    width = tokens_ref.shape[1]
    size = token_refs[0].shape[0]
    rows = pl.ds(pl.multiple_of(tile * TILE, TILE), TILE)
    lane = place_ref[0] + expert

    @pl.when(tile == 0)
    def _():
        base = 0
        for target, count in zip((gate, up, down), counts):
            assemble(target, order_ref, base, pieces[base : base + count])
            base += count

    @pl.when((expert == 0) & (tile == 0))
    def _():
        for i in range(blocks):
            at = slice(i * size, (i + 1) * size)
            tokens_ref[at, :] = token_refs[i][...]
            cots_ref[at, :] = cot_refs[i][:, :width]
            named[at, :] = cot_refs[i][:, width:]

    tokens = tokens_ref[rows, :]
    cots = cots_ref[rows, :]

    @pl.when(expert == 0)
    def _():
        logits = dot(tokens, router_ref[...])
        raised = jnp.where(named[rows, :] > 0.5, jnp.exp(logits), 0.0)
        gates_ref[rows, :] = raised / jnp.sum(raised, axis=1, keepdims=True)
        d_gates[rows, :] = jnp.zeros((TILE, LANES), F32)
        moe_sum[rows, :] = jnp.zeros((TILE, width), F32)
        back_sum[rows, :] = jnp.zeros((TILE, width), F32)

    chosen = lane_index((TILE, LANES)) == lane
    gates = jnp.sum(jnp.where(chosen, gates_ref[rows, :], 0.0), axis=1, keepdims=True)
    gate_act = dot(tokens, gate[...])
    up_act = dot(tokens, up[...])
    sigmoid = jax.nn.sigmoid(gate_act)
    silu = gate_act * sigmoid
    middle = silu * up_act
    gated = (gates * middle).astype(BF16)
    gated_ref[0] = gated
    moe_sum[rows, :] += dot(gated, down[...])
    plain = contract_last(cots, down[...])
    d_gate = jnp.sum(plain * middle, axis=1, keepdims=True)
    d_gates[rows, :] += jnp.where(chosen, d_gate, 0.0)
    d_middle = plain * gates
    d_gate_act = (d_middle * up_act * sigmoid * (1.0 + gate_act * (1.0 - sigmoid))).astype(BF16)
    d_up_act = (d_middle * silu).astype(BF16)
    d_gate_ref[0] = d_gate_act
    d_up_ref[0] = d_up_act
    back_sum[rows, :] += contract_last(d_gate_act, gate[...]) + contract_last(d_up_act, up[...])

    for i in range(blocks):
        at = slice(i * size, (i + 1) * size)

        @pl.when((expert == pl.num_programs(0) - 1) & (tile == i * size // TILE))
        def _():
            moe_refs[i][...] = moe_sum[at, :].astype(BF16)
            back_refs[i][:, :width] = back_sum[at, :].astype(BF16)
            whole = d_gates[at, :]
            high = whole.astype(BF16).astype(F32)
            back_refs[i][:, width:] = (
                high + pltpu.roll(whole - high, LANES // 2, 1)
            ).astype(BF16)


def experts(place, order, tokens, cots, router, *weights):
    blocks, (size, width) = len(tokens), tokens[0].shape
    count = blocks * size
    owned, _, hidden = weights[0][0].shape

    def whole(*shape):
        return pl.BlockSpec(shape, lambda e, t, *_: (0, 0))

    def expert(array):
        return pl.BlockSpec((1,) + array.shape[1:], lambda e, t, *_: (e, 0, 0))

    pieces = [piece for weight in weights for piece in weight]
    shapes = [(size, width)] * blocks + [(size, width + LANES)] * blocks + [(count, width)] * 2
    products = jax.ShapeDtypeStruct((owned, count, hidden), BF16)
    results = pl.pallas_call(
        functools.partial(
            experts_kernel, blocks=blocks, counts=[len(weight) for weight in weights]
        ),
        out_shape=[
            *(jax.ShapeDtypeStruct(shape, BF16) for shape in shapes),
            jax.ShapeDtypeStruct((count, LANES), F32),
            products, products, products,
        ],
        grid_spec=pltpu.PrefetchScalarGridSpec(
            num_scalar_prefetch=2,
            grid=(owned, count // TILE),
            in_specs=[
                *(whole(*block.shape) for block in tokens),
                *(whole(*block.shape) for block in cots),
                whole(*router.shape),
                *(expert(piece) for piece in pieces),
            ],
            out_specs=[
                *(whole(*shape) for shape in shapes),
                whole(count, LANES),
                *[pl.BlockSpec((1, TILE, hidden), lambda e, t, *_: (e, t, 0))] * 3,
            ],
            scratch_shapes=[
                pltpu.VMEM((count, LANES), BF16),
                pltpu.VMEM((width, hidden), BF16),
                pltpu.VMEM((width, hidden), BF16),
                pltpu.VMEM((hidden, width), BF16),
                pltpu.VMEM((count, width), F32),
                pltpu.VMEM((count, width), F32),
                pltpu.VMEM((count, LANES), F32),
            ],
        ),
        compiler_params=pltpu.CompilerParams(vmem_limit_bytes=60 << 20),
        cost_estimate=pl.CostEstimate(
            flops=12 * count * width * hidden * owned,
            bytes_accessed=6 * width * hidden * owned + 24 * count * width,
            transcendentals=count * hidden * owned,
        ),
    )(place, order, *tokens, *cots, router, *pieces)
    return results[:blocks], results[blocks : 2 * blocks], *results[2 * blocks :]


def spread_totals_kernel(order_ref, *refs, blocks):
    (query_ref, key_ref, value_ref, out_ref), parts = refs[blocks:], refs[:blocks]
    query, key = query_ref.shape[1], key_ref.shape[1]
    for i in range(blocks):

        @pl.when(pl.program_id(0) == i)
        def _():
            block = parts[i][...].astype(F32)
            query_ref[...] = block[:, :query]
            key_ref[...] = block[:, query : query + key]
            value_ref[...] = block[:, query + key : query + 2 * key]
            out_ref[...] = block[:, query + 2 * key :]


def spread_totals(order, parts, query, key):
    blocks, share = len(parts), parts[0].shape[0]

    def rows(columns):
        return pl.BlockSpec((share, columns), lambda i, o: (o[i], 0))

    columns = parts[0].shape[1] - query - 2 * key
    return pl.pallas_call(
        functools.partial(spread_totals_kernel, blocks=blocks),
        out_shape=[
            jax.ShapeDtypeStruct((blocks * share, query), F32),
            jax.ShapeDtypeStruct((blocks * share, key), F32),
            jax.ShapeDtypeStruct((blocks * share, key), F32),
            jax.ShapeDtypeStruct((share, blocks * columns), F32),
        ],
        grid_spec=pltpu.PrefetchScalarGridSpec(
            num_scalar_prefetch=1,
            grid=(blocks,),
            in_specs=[pl.BlockSpec(part.shape, lambda i, o: (0, 0)) for part in parts],
            out_specs=[
                rows(query), rows(key), rows(key),
                pl.BlockSpec((share, columns), lambda i, o: (0, o[i])),
            ],
        ),
        compiler_params=pltpu.CompilerParams(vmem_limit_bytes=40 << 20),
        cost_estimate=pl.CostEstimate(
            flops=0, bytes_accessed=6 * blocks * parts[0].size, transcendentals=0
        ),
    )(order, *parts)


def shares_kernel(order_ref, *refs, groups, entries, added):
    for i in range(entries):
        total = None
        for group in range(groups):
            start = group * (entries + 1)
            left, right = refs[start + i], refs[start + entries]
            left = left[...] if len(left.shape) == 2 else left[0]
            right = right[...] if len(right.shape) == 2 else right[0]
            part = contract_first(left, right)
            total = part if total is None else total + part
        if added:
            total = total + refs[groups * (entries + 1)][i, 0].astype(F32)
        refs[-1][i, 0] = total.astype(BF16)


def shares(order, groups, rows, added=None):
    entries = order.shape[0]
    specs, operands = [], []
    for left, right in groups:
        for i in range(entries):
            if left.ndim == 2:
                specs.append(pl.BlockSpec((left.shape[0], rows), lambda e, o, i=i: (0, o[i])))
            else:
                specs.append(
                    pl.BlockSpec((1, left.shape[1], rows), lambda e, o, i=i: (e, 0, o[i]))
                )
            operands.append(left)
        if right.ndim == 2:
            specs.append(pl.BlockSpec(right.shape, lambda e, o: (0, 0)))
        else:
            specs.append(pl.BlockSpec((1,) + right.shape[1:], lambda e, o: (e, 0, 0)))
        operands.append(right)
    owned = max(array.shape[0] for array in groups[0] if array.ndim == 3)
    columns = groups[0][1].shape[-1]
    block = pl.BlockSpec((entries, 1, rows, columns), lambda e, o: (0, e, 0, 0))
    if added is not None:
        specs.append(block)
        operands.append(added)
    tokens = sum(left.shape[-2] for left, _ in groups)
    return pl.pallas_call(
        functools.partial(
            shares_kernel, groups=len(groups), entries=entries, added=added is not None
        ),
        out_shape=jax.ShapeDtypeStruct((entries, owned, rows, columns), BF16),
        grid_spec=pltpu.PrefetchScalarGridSpec(
            num_scalar_prefetch=1, grid=(owned,), in_specs=specs, out_specs=block
        ),
        compiler_params=pltpu.CompilerParams(vmem_limit_bytes=40 << 20),
        cost_estimate=pl.CostEstimate(
            flops=2 * tokens * rows * columns * owned * entries,
            bytes_accessed=4 * owned * entries * rows * columns + 6 * tokens * columns * owned,
            transcendentals=0,
        ),
    )(order, *operands)


def rotate(tensor, cosine_table, sine_table):
    half_size = tensor.shape[-1] // 2
    first = tensor[..., :half_size]
    second = tensor[..., half_size:]
    return jnp.concatenate(
        [first * cosine_table - second * sine_table, second * cosine_table + first * sine_table],
        axis=-1,
    )


def plain_scores(query_rows, key_rows):
    scores = (
        jnp.einsum("skgqd,skvd->skgqv", query_rows, key_rows, preferred_element_type=F32) * SCALE
    )
    positions = jnp.arange(SEQUENCE_TOKENS, dtype=jnp.int32)
    causal = positions[:, None] >= positions[None, :]
    total = jnp.sum(jnp.where(causal, jnp.exp(scores), 0.0), axis=-1, keepdims=True)
    return jnp.where(causal, jnp.exp(scores - jnp.log(total)), 0.0)


def plain_forward(normed_all, joined, w_out):
    query_width = w_out.shape[0]
    kv_local = query_width // GROUP // HEAD_SIZE
    cosine_table, sine_table = rope_tables()
    projected = dot(normed_all, joined)
    split = (-1, SEQUENCE_TOKENS, kv_local)
    query = projected[:, :query_width].reshape(*split, GROUP, HEAD_SIZE).transpose(0, 2, 3, 1, 4)
    key, value = (
        part.reshape(*split, HEAD_SIZE).transpose(0, 2, 1, 3)
        for part in jnp.split(projected[:, query_width:], 2, axis=1)
    )
    value = value.astype(BF16)
    query = rotate(query, cosine_table, sine_table).astype(BF16)
    key = rotate(key, cosine_table, sine_table).astype(BF16)
    probs = plain_scores(query, key).astype(BF16)
    heads = jnp.einsum("skgqv,skvd->skgqd", probs, value, preferred_element_type=F32)
    heads = heads.astype(BF16).transpose(0, 3, 1, 2, 4).reshape(-1, query_width)
    return dot(heads, w_out), query, key, value, heads


def plain_backward(d_attn_all, w_out, query, key, value):
    query_width = w_out.shape[0]
    rows = d_attn_all.shape[0]
    kv_local = query_width // GROUP // HEAD_SIZE
    cosine_table, sine_table = rope_tables()
    grad = contract_last(d_attn_all, w_out).astype(BF16)
    grad = grad.reshape(-1, SEQUENCE_TOKENS, kv_local, GROUP, HEAD_SIZE).transpose(0, 2, 3, 1, 4)
    probs = plain_scores(query, key)
    d_value = jnp.einsum(
        "skgqv,skgqd->skvd", probs.astype(BF16), grad, preferred_element_type=F32
    )
    d_probs = jnp.einsum("skgqd,skvd->skgqv", grad, value, preferred_element_type=F32)
    d_scores = (
        probs * (d_probs - jnp.sum(probs * d_probs, axis=-1, keepdims=True)) * SCALE
    ).astype(BF16)
    d_query = jnp.einsum("skgqv,skvd->skgqd", d_scores, key, preferred_element_type=F32)
    d_key = jnp.einsum("skgqv,skgqd->skvd", d_scores, query, preferred_element_type=F32)
    d_query = rotate(d_query, cosine_table, -sine_table).astype(BF16).transpose(0, 3, 1, 2, 4)
    d_key = rotate(d_key, cosine_table, -sine_table).astype(BF16).transpose(0, 2, 1, 3)
    d_value = d_value.astype(BF16).transpose(0, 2, 1, 3)
    return jnp.concatenate([part.reshape(rows, -1) for part in (d_query, d_key, d_value)], axis=1)


def normalize(row_data):
    inverse = lax.rsqrt(jnp.mean(row_data * row_data, axis=-1, keepdims=True) + EPS)
    return (row_data * inverse, inverse)


def normalize_back(d_normed, normal_hat, inverse, gain):
    d_hat = d_normed * gain
    return inverse * (d_hat - normal_hat * jnp.mean(d_hat * normal_hat, axis=-1, keepdims=True))


def after(value, *earlier):
    return lax.optimization_barrier((value, *earlier))[0] if earlier else value


def add(*parts):
    return sum(part.astype(F32) for part in parts)


class Axis:
    def __init__(self, name, size):
        self.name = name
        self.size = size
        self.mine = lax.axis_index(name)

    def fetch(self, value, distance):
        n = self.size
        return lax.ppermute(value, self.name, [((i + distance) % n, i) for i in range(n)])

    def deliver(self, value, distance):
        n = self.size
        return lax.ppermute(value, self.name, [(i, (i + distance) % n) for i in range(n)])


class Tensor:
    def __init__(self, size):
        self.size = size
        self.halves = size // 2
        self.mine = lax.axis_index("tensor")
        self.half = self.mine // 2
        self.core = self.mine % 2

    def swap_core(self, value):
        return lax.ppermute(value, "tensor", [(t, t ^ 1) for t in range(self.size)])

    def shift_half(self, value, step):
        n = self.halves
        return lax.ppermute(
            value, "tensor", [(t, (t // 2 + step) % n * 2 + t % 2) for t in range(self.size)]
        )

    def order(self):
        places = []
        for step in range(self.halves):
            half = (self.half - step) % self.halves
            places += [half * 2 + self.core, half * 2 + 1 - self.core]
        return places

    def gather(self, value):
        mine = [value] + [self.shift_half(value, step) for step in range(1, self.halves)]
        pieces = [piece for one in mine for piece in (one, self.swap_core(one))]
        out = jnp.zeros((self.size,) + value.shape, value.dtype)
        for place, piece in zip(self.order(), pieces):
            out = lax.dynamic_update_slice(out, piece[None], (place,) + (0,) * value.ndim)
        return out

    def scatter(self, stacked):
        n = self.halves
        view = stacked.reshape((n, 2) + stacked.shape[1:])
        kept = lax.dynamic_index_in_dim(view, self.core, 1, keepdims=False)
        given = lax.dynamic_index_in_dim(view, 1 - self.core, 1, keepdims=False)
        pair = add(kept, self.swap_core(given))
        total = lax.dynamic_index_in_dim(pair, self.half, 0, keepdims=False)
        for step in range(1, n):
            part = lax.dynamic_index_in_dim(pair, (self.half + step) % n, 0, keepdims=False)
            total = add(total, self.shift_half(part.astype(BF16), step))
        return total


def swap_all(value, sizes):
    for axis, size in sizes:
        bit = 1
        while bit < size:
            value = value + lax.ppermute(value, axis, [(i, i ^ bit) for i in range(size)])
            bit *= 2
    return value


def fetch_weight(ring, copies, weight):
    size = weight.shape[1] // copies.size
    part = lax.dynamic_slice_in_dim(weight, copies.mine * size, size, 1)
    pieces = [(weight, ring.half, 1, 0)]
    for step in range(1, ring.halves):
        got = ring.shift_half(part, step)
        half = (ring.half - step) % ring.halves
        pieces.append((got, half, copies.size, copies.mine))
        for k in range(1, copies.size):
            other = (copies.mine + k) % copies.size
            pieces.append((copies.fetch(got, k), half, copies.size, other))
    arrays, places = [], []
    for core, swap in ((ring.core, False), (1 - ring.core, True)):
        for array, half, parts, part in pieces:
            arrays.append(ring.swap_core(array) if swap else array)
            places.append((half * 2 + core) * parts + part)
    return arrays, places


def shared_grads(ring, groups, rows):
    order = ring.order()

    def part(places, added):
        if rows % LANES == 0:
            return shares(jnp.stack(places).astype(jnp.int32), groups, rows, added)
        blocks = []
        for place in places:
            total = None
            for left, right in groups:
                left = lax.dynamic_slice_in_dim(left, place * rows, rows, left.ndim - 1)
                sums = "td,etf->edf" if left.ndim == 2 else "etd,tf->edf"
                one = jnp.einsum(sums, left, right, preferred_element_type=F32)
                total = one if total is None else total + one
            blocks.append(total)
        stacked = jnp.stack(blocks)
        return (stacked if added is None else add(stacked, added)).astype(BF16)

    given = part(order[1::2], None)
    return part(order[0::2], ring.swap_core(given))


def local(
    sizes,
    layer_input,
    norm1_gain,
    w_query,
    key_matrix,
    value_matrix,
    w_out,
    norm2_gain,
    w_router,
    w_gate,
    w_up,
    w_down,
    routes,
    cotangent,
):
    row_count, width = layer_input.shape
    expert_total = w_router.shape[1]
    owned = w_gate.shape[0]
    ring = Tensor(sizes["tensor"])
    line = Axis("expert", sizes["expert"])
    copies = Axis("dp", sizes["dp"])
    query_width = w_query.shape[1]
    kv_width = key_matrix.shape[1]
    by_kernel = (
        2 * row_count == SEQUENCE_TOKENS and query_width % LANES == 0 and kv_width == LANES
    )
    core = ring.core.astype(jnp.int32)[None]

    row_float = layer_input.astype(F32)
    hat_one, inverse_one = normalize(row_float)
    normed_one = (hat_one * norm1_gain).astype(BF16)
    weights = (w_query, key_matrix, value_matrix)
    tables = lane_tables()
    named = jnp.sum(
        (routes[:, :, None] == jnp.arange(LANES, dtype=jnp.int32)).astype(BF16), axis=1
    )
    cots = jnp.concatenate([cotangent, named], axis=1)
    cots_of = {k: line.fetch(cots, k) if k else cots for k in range(line.size)}
    if by_kernel:
        partner = ring.swap_core(normed_one)
        across = ring.shift_half(normed_one, 1)
        across_partner = ring.swap_core(across)
        down_pieces, down_places = fetch_weight(ring, copies, w_down)
        near = attention_forward(core, normed_one, partner, weights, w_out, tables)
        far = attention_forward(core, across, across_partner, weights, w_out, tables)
        far_sum = add(far[0], ring.swap_core(far[1])).astype(BF16)
        attended = add(near[0], ring.swap_core(near[1]), ring.shift_half(far_sum, 1))
    else:
        normed_all = ring.gather(normed_one).reshape(-1, width)
        down_pieces, down_places = fetch_weight(ring, copies, w_down)
        joined = jnp.concatenate(weights, axis=1)
        attended, query, key, value, heads = plain_forward(normed_all, joined, w_out)
        attended = ring.scatter(attended.reshape(ring.size, row_count, width))
    hidden = row_float + attended

    hat_two, inverse_two = normalize(hidden)
    normed_two = (hat_two * norm2_gain).astype(BF16)
    gate_pieces, gate_places = fetch_weight(ring, copies, w_gate)
    up_pieces, up_places = fetch_weight(ring, copies, w_up)
    order = jnp.stack(gate_places + up_places + down_places).astype(jnp.int32)
    tokens_of = {k: line.fetch(normed_two, k) if k else normed_two for k in range(line.size)}
    router = jnp.pad(w_router, ((0, 0), (0, LANES - expert_total)))
    place = (line.mine * owned).astype(jnp.int32)[None]

    moe_of, back_of, token_groups, cot_groups, products = {}, {}, [], [], []
    early, late = list(range(1, line.size - 1)), [line.size - 1, 0]
    for group in (early, late):
        moe, back, rows, grads, gates_group, *made = experts(
            place, order, [tokens_of[k] for k in group], [cots_of[k] for k in group],
            router, gate_pieces, up_pieces, down_pieces,
        )
        if 0 in group:
            at = group.index(0) * row_count
            gates = gates_group[at : at + row_count]
        moe_of.update(zip(group, moe))
        back_of.update(zip(group, back))
        token_groups.append(rows)
        cot_groups.append(grads)
        products.append(made)
    backs = [back_of[0]] + [line.deliver(back_of[k], k) for k in range(1, line.size)]
    back = add(*backs)
    d_normed_two = back[:, :width]
    d_gates = back[:, width : width + LANES // 2] + back[:, width + LANES // 2 :]
    gated, d_gate_act, d_up_act = ([made[i] for made in products] for i in range(3))
    gate_kept = shared_grads(ring, list(zip(token_groups, d_gate_act)), w_gate.shape[1])
    up_kept = shared_grads(ring, list(zip(token_groups, d_up_act)), w_up.shape[1])
    down_kept = shared_grads(ring, list(zip(gated, cot_groups)), w_down.shape[1])

    gates = gates[:, : LANES // 2]
    d_logits = (gates * (d_gates - jnp.sum(gates * d_gates, axis=-1, keepdims=True))).astype(BF16)
    grad_router = contract_first(d_logits, normed_two)[:expert_total]
    d_normed_two = d_normed_two + contract_last(d_logits, router[:, : LANES // 2])
    grad_norm2 = jnp.sum(d_normed_two * hat_two, axis=0)
    d_hidden = cotangent.astype(F32) + normalize_back(
        d_normed_two, hat_two, inverse_two, norm2_gain
    )

    d_attn = d_hidden.astype(BF16)
    if by_kernel:
        d_partner = ring.swap_core(d_attn)
        d_across = ring.shift_half(d_attn, 1)
        d_across_partner = ring.swap_core(d_across)
        near_back = attention_backward(core, d_attn, d_partner, weights, w_out, tables, *near[3:6])
        far_back = attention_backward(
            core, d_across, d_across_partner, weights, w_out, tables, *far[3:6]
        )
        grad_out = contract_first(near[6], near_back[2]) + contract_first(far[6], far_back[2])
        grad_joined = contract_first(near[2], near_back[3]) + contract_first(far[2], far_back[3])
        grad_joined, grad_out = grad_joined.astype(BF16), grad_out.astype(BF16)
        far_given = after(far_back[1], grad_joined, grad_out)
        far_sum = add(far_back[0], ring.swap_core(far_given)).astype(BF16)
        d_normed_one = add(near_back[0], ring.swap_core(near_back[1]), ring.shift_half(far_sum, 1))
    else:
        d_attn_all = ring.gather(d_attn).reshape(-1, width)
        d_projected = plain_backward(d_attn_all, w_out, query, key, value)
        d_normed_one = ring.scatter(
            contract_last(d_projected, joined).reshape(ring.size, row_count, width)
        )
        grad_out = contract_first(heads, d_attn_all).astype(BF16)
        grad_joined = contract_first(normed_all, d_projected).astype(BF16)
    grad_norm1 = jnp.sum(d_normed_one * hat_one, axis=0)
    d_input = d_hidden + normalize_back(d_normed_one, hat_one, inverse_one, norm1_gain)

    share = width // line.size
    joined_width = grad_joined.shape[1]

    def shared(k):
        at = (line.mine + k) % line.size * share
        return jnp.concatenate(
            [
                lax.dynamic_slice_in_dim(grad_joined, at, share, 0),
                lax.dynamic_slice_in_dim(grad_out, at, share, 1),
            ],
            axis=1,
        )

    parts = [shared(0)] + [line.deliver(shared(k), k) for k in range(1, line.size)]
    part = add(*parts).astype(BF16)
    for k in range(1, copies.size):
        part = add(part, copies.fetch(part, k)).astype(BF16)
    shares_of = [part] + [line.fetch(part, k) for k in range(1, line.size)]
    places = jnp.stack([(line.mine + k) % line.size for k in range(line.size)]).astype(jnp.int32)
    if kv_width % LANES == 0:
        grad_query, grad_key, grad_value, grad_out = spread_totals(
            places, shares_of, query_width, kv_width
        )
    else:
        grad_joined = jnp.zeros((width, joined_width), F32)
        grad_out = jnp.zeros((query_width, width), F32)
        for k, got in enumerate(shares_of):
            got, at = got.astype(F32), places[k] * share
            grad_joined = lax.dynamic_update_slice_in_dim(grad_joined, got[:, :joined_width], at, 0)
            grad_out = lax.dynamic_update_slice_in_dim(grad_out, got[:, joined_width:], at, 1)
        grad_query = grad_joined[:, :query_width]
        grad_key = grad_joined[:, query_width : query_width + kv_width]
        grad_value = grad_joined[:, query_width + kv_width :]
    moes = [moe_of[0]] + [line.deliver(moe_of[k], k) for k in range(1, line.size)]
    layer_output = (hidden + add(*moes)).astype(BF16)

    pad = -(expert_total + 2) % 16
    small = jnp.concatenate([grad_router, grad_norm2[None], grad_norm1[None]], axis=0)
    small = jnp.pad(small, ((0, pad), (0, 0)))
    small = small + ring.swap_core(small)
    small = swap_all(small, [("expert", line.size)])
    if ring.halves > 2:
        bits = [1 << i for i in range(1, ring.halves.bit_length())]
        for bit in bits:
            small = small + lax.ppermute(small, "tensor", [(t, t ^ bit) for t in range(ring.size)])

    def over_halves(kept, rider=None):
        total, riders = kept[0], []
        for step in range(1, ring.halves):
            part = kept[step]
            shape = part.shape
            if rider is not None:
                part = jnp.concatenate([part.reshape(-1, width), rider], axis=0)
            got = ring.shift_half(part, ring.halves - step)
            if rider is not None:
                riders.append(got[-rider.shape[0] :])
                got = got[: -rider.shape[0]].reshape(shape)
            total = add(total, got)
        return total.astype(BF16), riders

    def over_copies(total):
        for k in range(1, copies.size):
            total = add(total, copies.fetch(total, k))
        return total.astype(F32)

    cut = owned // 2
    low = small.astype(BF16)
    gate_first, _ = over_halves(gate_kept[:, :cut])
    gate_second, _ = over_halves(gate_kept[:, cut:])
    up_total, _ = over_halves(up_kept)
    down_first, riders = over_halves(down_kept[:, cut:], low if ring.halves == 2 else None)
    down_second, _ = over_halves(down_kept[:, :cut])
    if riders:
        low = add(low, riders[0]).astype(BF16)
    grad_gate = jnp.concatenate([over_copies(gate_first), over_copies(gate_second)], axis=0)
    grad_up = over_copies(up_total)
    shape = down_first.shape
    mixed = over_copies(jnp.concatenate([down_first.reshape(-1, width), low], axis=0))
    grad_down = jnp.concatenate(
        [over_copies(down_second), mixed[: -low.shape[0]].reshape(shape)], axis=0
    )
    small = mixed[-low.shape[0] :]
    return (
        layer_output,
        d_input,
        small[expert_total + 1],
        grad_query,
        grad_key,
        grad_value,
        grad_out,
        small[expert_total],
        small[:expert_total].T,
        grad_gate,
        grad_up,
        grad_down,
    )


def solution(mesh):
    in_specs = (
        P(("dp", "expert", "tensor"), None),
        P(),
        P(None, "tensor"),
        P(None, "tensor"),
        P(None, "tensor"),
        P("tensor", None),
        P(),
        P(),
        P("expert", "tensor", None),
        P("expert", "tensor", None),
        P("expert", "tensor", None),
        P(("dp", "expert", "tensor"), None),
        P(("dp", "expert", "tensor"), None),
    )
    out_specs = (
        P(("dp", "expert", "tensor"), None),
        P(("dp", "expert", "tensor"), None),
        P(),
        P(None, "tensor"),
        P(None, "tensor"),
        P(None, "tensor"),
        P("tensor", None),
        P(),
        P(),
        P("expert", "tensor", None),
        P("expert", "tensor", None),
        P("expert", "tensor", None),
    )

    def step(*args):
        return local(dict(mesh.shape), *args)

    return jax.shard_map(
        step, mesh=mesh, in_specs=in_specs, out_specs=out_specs, check_vma=False
    )
```
